512 devices in a mesh: ev: 32 (over x, y_lo, core), ch: 16 (over y_hi, z).
Axes of the slice: x: 4, y: 8 (y_hi: 2, y_lo: 4; y = y_hi * 4 + y_lo), z: 8, core: 2. Of those that a mesh axis runs over, the one named last changes fastest.
Arguments:
- spectra: float32 [512, 16, 65536], P('ev', None, 'ch'), as said below
- tile_mask: int32 [512, 512], P('ev', 'ch'), may hold values 0 or 1
- source_init: float32 [512, 16], P('ev'), may hold values from -6 to 6
- site_init: float32 [16, 65536], P(None, 'ch'), may hold values from -6 to 6
- event_pos: float32 [3, 512], P(None, 'ev'), may hold values from 5 to 50
- channel_pos: float32 [2, 65536], P(None, 'ch'), may hold values from 0 to 50
- atten: float32 [16], replicated, may hold values from 0.02 to 0.3
Outputs:
- source: float32 [512, 16], P('ev')
- site: float32 [16, 65536], P(None, 'ch')
The draws below stay inside these ranges and needn't reach their ends.
Inputs may be any that keep to these rules, and one draw needn't show every extreme that they name: spectra are log amplitudes of order one to a few, with outliers. `tile_mask`: 0 marks an event invalid on a whole tile of 128 channels.
All inputs are finite; a program needn't handle non-finite values. No bound on the sum of `tile_mask` on one device may be relied on, other than what follows from the above.
Results may differ from the reference program's by a relative error of at most 0.0001.
Values sent between devices are 32-bit elements; how exact they have to be, the bound alone decides.
A program may use at most 64 MiB of HBM per device.

```python
import math
import jax
import jax.numpy as jnp
from jax import lax

EV_DEV = 16
FREQS = 16
ITERS = 2
EVENTS = 512
CHANNELS = 65536


def draw_spectra(key, part):
    keys = jax.random.split(key, 7)
    src_true = 2.0 * jax.random.normal(keys[0], (EVENTS, FREQS, 1), jnp.float32)
    site_true = jax.random.normal(keys[1], (1, FREQS, CHANNELS), jnp.float32)
    ev_scale = jnp.exp(jax.random.uniform(keys[2], (EVENTS, 1, 1), jnp.float32) * 2.302585)
    ch_scale = jnp.exp(jax.random.uniform(keys[3], (1, 1, CHANNELS), jnp.float32) * 2.302585)
    outlier = jax.random.bernoulli(keys[5], 0.05, (EVENTS, FREQS, CHANNELS)).astype(jnp.float32)
    sign = jnp.where(jax.random.bernoulli(keys[6], 0.5, (EVENTS, FREQS, CHANNELS)), 1.0, -1.0)
    noise = jax.random.normal(keys[4], (EVENTS, FREQS, CHANNELS), jnp.float32)
    noise = jnp.clip(noise, -4.0, 4.0)
    return src_true + site_true + 0.05 * ev_scale * ch_scale * noise + 6.0 * outlier * sign


def with_ends(result, key, low, high):
    longest = result.shape.index(max(result.shape))
    spots = []
    for shift in (0, 1):
        where = [jax.random.randint(jax.random.fold_in(key, axis), (), 0, length) for axis, length in enumerate(result.shape)]
        where[longest] = (where[longest] + shift) % result.shape[longest]
        spots.append(tuple(where))
    return result.at[spots[0]].set(low).at[spots[1]].set(high)


def level_of(rng, dims, cuts, least, largest):
    level, own = 1.0, jax.random.fold_in(rng, 6)
    for dim, shards_of in cuts:
        draws = jnp.exp(jax.random.uniform(jax.random.fold_in(own, dim), (shards_of,), jnp.float32, least / len(cuts), largest / len(cuts)))
        level = level * jnp.repeat(draws, dims[dim] // shards_of).reshape([-1 if axis == dim else 1 for axis in range(len(dims))])
    return level


def normal_values(own_key, shape, deviation, most, pieces=(), held_as=jnp.bfloat16):
    result = jax.random.normal(own_key, shape, jnp.float32) * deviation
    if len(pieces) > 0:
        result = level_of(own_key, shape, pieces, -0.22, 0.18) * result
    return jnp.clip(result, min=-most, max=most).astype(held_as)


def setup_inputs(seed: int = 0) -> dict:
    seeds = jax.random.split(jax.random.key(seed), 8)
    spectra = draw_spectra(jax.random.fold_in(seeds[7], 71), 0)
    tile_mask = with_ends((jax.random.randint(seeds[1], (EVENTS, CHANNELS // 128), 0, 8) < 7).astype(jnp.int32), jax.random.fold_in(seeds[1], 1), 0, 1)
    source_init = normal_values(seeds[2], (EVENTS, FREQS), 1.0, 6.0, ((0, 32),), jnp.float32)
    site_init = normal_values(seeds[3], (FREQS, CHANNELS), 1.0, 6.0, ((1, 16),), jnp.float32)
    event_pos = jnp.clip(5.0 + 45.0 * jax.random.uniform(seeds[4], (3, EVENTS), jnp.float32) ** level_of(seeds[4], (3, EVENTS), ((1, 32),), -0.2, 0.2), 5.0, 50.0)
    channel_pos = jnp.clip(50.0 * jax.random.uniform(seeds[5], (2, CHANNELS), jnp.float32) ** level_of(seeds[5], (2, CHANNELS), ((1, 16),), -0.2, 0.2), 0.0, 50.0)
    atten = jnp.clip(jnp.exp(jax.random.uniform(seeds[6], (FREQS,), jnp.float32, math.log(0.02), math.log(0.3))), 0.02, 0.3)
    return dict(spectra=spectra, tile_mask=tile_mask, source_init=source_init, site_init=site_init, event_pos=event_pos, channel_pos=channel_pos, atten=atten)


def residual_block(spec, mask, src, site, pos, channel_pos, atten):
    east = pos[0][:, None] - channel_pos[0][None, :]
    north = pos[1][:, None] - channel_pos[1][None, :]
    depth = pos[2][:, None]
    travel = jnp.sqrt(east * east + north * north + depth * depth) / 3.0
    resid = spec - src[:, :, None] - site[None, :, :] + atten[None, :, None] * travel[:, None, :]
    valid = jnp.repeat(mask, 128, axis=1).astype(jnp.float32)[:, None, :]
    return (resid, valid)

def reference(spectra, tile_mask, source_init, site_init, event_pos, channel_pos, atten):
    blocks = EVENTS // EV_DEV
    spec_b = spectra.reshape(blocks, EV_DEV, FREQS, CHANNELS)
    mask_b = tile_mask.reshape(blocks, EV_DEV, CHANNELS // 128)
    pos_b = event_pos.reshape(3, blocks, EV_DEV).transpose(1, 0, 2)
    source = source_init
    site = site_init
    for step in range(ITERS):
        src_b = source.reshape(blocks, EV_DEV, FREQS)

        def stat_step(carry, xs):
            spec, mask, srcb, pos = xs
            resid, valid = residual_block(spec, mask, srcb, site, pos, channel_pos, atten)
            return ((carry[0] + lax.optimization_barrier(jnp.sum(valid * jnp.abs(resid), axis=(0, 2))), carry[1] + jnp.sum(valid)), None)
        init = (jnp.zeros((FREQS,), jnp.float32), jnp.zeros((), jnp.float32))
        (absum, count), _ = lax.scan(stat_step, init, (spec_b, mask_b, src_b, pos_b))
        delta = 1.345 * (1.2533 * absum / jnp.maximum(count, 1.0) + 1e-05)

        def weight_step(carry, xs):
            spec, mask, srcb, pos = xs
            resid, valid = residual_block(spec, mask, srcb, site, pos, channel_pos, atten)
            limit = delta[None, :, None]
            weight = limit / jnp.maximum(jnp.abs(resid), limit) * valid
            product = weight * resid
            return ((carry[0] + lax.optimization_barrier(jnp.sum(product, axis=0)), carry[1] + lax.optimization_barrier(jnp.sum(weight, axis=0))), (lax.optimization_barrier(jnp.sum(product, axis=2)), lax.optimization_barrier(jnp.sum(weight, axis=2))))
        zeros_site = jnp.zeros((FREQS, CHANNELS), jnp.float32)
        (site_num, site_den), (src_num, src_den) = lax.scan(weight_step, (zeros_site, zeros_site), (spec_b, mask_b, src_b, pos_b))
        source = source + 0.5 * src_num.reshape(EVENTS, FREQS) / (src_den.reshape(EVENTS, FREQS) + 1.0)
        site = site + 0.5 * site_num / (site_den + 1.0)
        shift = lax.optimization_barrier(jnp.sum(site, axis=1)) / CHANNELS
        site = site - shift[:, None]
        source = source + shift[None, :]
    return (source, site)
```

```python
import functools
import jax
import jax.numpy as jnp
from jax import lax
from jax.experimental import pallas as pl
from jax.experimental.pallas import tpu as pltpu
from jax.sharding import PartitionSpec as P

ITERS = 2
LANES = 128
X, Y_LO, CORE, Y_HI, Z = 4, 4, 2, 2, 8
Y = Y_HI * Y_LO
CHIPS = X * Y_LO
f32 = jnp.float32


def ring(step, size):
    return min(step, size - step)


STAGE_A = sorted(
    ((dz, dc) for dz in range(Z) for dc in range(CORE) if dz or dc),
    key=lambda s: -ring(s[0], Z),
)
STAGE_B = sorted(
    ((dy, dx) for dy in range(Y) for dx in range(X) if dy or dx),
    key=lambda s: -ring(s[0], Y) - ring(s[1], X),
)
GROUP = sorted(
    ((dx, dy) for dx in range(X) for dy in range(Y_LO) if dx or dy),
    key=lambda s: -ring(s[0], X) - (0, 1.5, 2, 1.5)[s[1]],
)
CHAN = sorted(
    ((dh, dz) for dh in range(Y_HI) for dz in range(Z) if dh or dz),
    key=lambda s: -4 * s[0] - ring(s[1], Z),
)


def kernel(
    spectra, mask_h, source_h, site_h, event_h, channel_h, atten_h,
    source_o, site_o,
    rbuf, site, chan, srcv, attv, maskv, mask, evp, chx, srcb, dsb, sn, sd,
    away, recv_s, own, recv_c, gath, bsend, brecv, arow, arecv_a, arecv_b,
    spec_sem, in_sem, s_send, s_recv, c_send, c_recv, g_send, g_recv, f_send, f_recv,
    b_send, b_recv, aa_send, aa_recv, ab_send, ab_recv,
):
    n_ev, freqs, n_ch = rbuf.shape
    tiles = n_ch // LANES
    half = tiles // 2
    ev, ch = lax.axis_index("ev"), lax.axis_index("ch")
    core, chip = lax.rem(ev, CORE), ev // CORE
    x, y_lo = chip // Y_LO, lax.rem(chip, Y_LO)
    y_hi, z = ch // Z, lax.rem(ch, Z)
    y = y_hi * Y_LO + y_lo

    def place(px, py, pz, pc):
        return ((px * Y_LO + lax.rem(py, Y_LO)) * CORE + pc, (py // Y_LO) * Z + pz)

    stage_a = [place(x, y, lax.rem(z + dz, Z), lax.rem(core + dc, CORE)) for dz, dc in STAGE_A]
    stage_b = [place(lax.rem(x + dx, X), lax.rem(y + dy, Y), z, core) for dy, dx in STAGE_B]
    group_chip = [lax.rem(x + dx, X) * Y_LO + lax.rem(y_lo + dy, Y_LO) for dx, dy in GROUP]
    group_from = [lax.rem(x + X - dx, X) * Y_LO + lax.rem(y_lo + Y_LO - dy, Y_LO) for dx, dy in GROUP]
    group = [(g * CORE + core, ch) for g in group_chip]
    sibling = (chip * CORE + 1 - core, ch)
    chan_peers = [(ev, lax.rem(y_hi + dh, Y_HI) * Z + lax.rem(z + dz, Z)) for dh, dz in CHAN]

    def remote(src, dst, send, recv, peer):
        return pltpu.make_async_remote_copy(
            src_ref=src, dst_ref=dst, send_sem=send, recv_sem=recv,
            device_id=peer, device_id_type=pl.DeviceIdType.MESH,
        )

    def spec_copy(e):
        return pltpu.make_async_copy(spectra.at[e], rbuf.at[e], spec_sem.at[e])

    small = [
        pltpu.make_async_copy(src, dst, in_sem.at[i])
        for i, (src, dst) in enumerate(
            [(mask_h, mask), (event_h, evp), (channel_h, chan), (atten_h, attv),
             (source_h, srcv), (mask_h, maskv), (site_h, site)]
        )
    ]
    for copy in small:
        copy.start()

    @pl.loop(0, n_ev)
    def _(e):
        spec_copy(e).start()

    barrier = pltpu.get_barrier_semaphore()
    for peer in stage_a + stage_b:
        pl.semaphore_signal(barrier, inc=1, device_id=peer, device_id_type=pl.DeviceIdType.MESH)

    shape = (freqs, LANES)
    rows = lax.broadcasted_iota(jnp.int32, shape, 0)
    lanes = lax.broadcasted_iota(jnp.int32, shape, 1)
    diag = rows == lanes

    def to_column(row):
        spread = jnp.where(diag, jnp.broadcast_to(row, shape), 0.0)
        return jnp.sum(spread, axis=1, keepdims=True)

    def to_row(column):
        spread = jnp.where(diag, jnp.broadcast_to(column, shape), 0.0)
        return jnp.sum(spread, axis=0, keepdims=True)

    pending = []

    def all_sum(phase, row):
        arow[phase, 0] = row
        for stage, peers, landed, send, recv in (
            (0, stage_a, arecv_a, aa_send, aa_recv),
            (1, stage_b, arecv_b, ab_send, ab_recv),
        ):
            copies = [
                remote(arow.at[phase, stage], landed.at[phase, k], send.at[phase, k], recv.at[phase, k], peer)
                for k, peer in enumerate(peers)
            ]
            for copy in copies:
                copy.start()
            total = row
            for k, copy in enumerate(copies):
                copy.wait_recv()
            parts = [row] + [landed[phase, k] for k in range(len(peers))]
            while len(parts) > 1:
                parts = [a + b for a, b in zip(parts[::2], parts[1::2])] + parts[len(parts) // 2 * 2:]
            row = parts[0]
            if stage == 0:
                arow[phase, 1] = row
            pending.extend(copies)
        return row

    for copy in small:
        copy.wait()

    small_shape = (n_ev, freqs)
    small_diag = lax.broadcasted_iota(jnp.int32, small_shape, 0) == lax.broadcasted_iota(jnp.int32, small_shape, 1)

    def widen(row):
        spread = jnp.where(small_diag, jnp.broadcast_to(row, small_shape), 0.0)
        return jnp.broadcast_to(jnp.sum(spread, axis=1, keepdims=True), shape)

    for t in range(tiles):
        chx[0, t:t + 1, :] = chan[0:1, t * LANES:(t + 1) * LANES]
        chx[1, t:t + 1, :] = chan[1:2, t * LANES:(t + 1) * LANES]
    for e in range(n_ev):
        srcb[e] = widen(srcv[e:e + 1, :])
    attb = widen(attv[0:1, :])
    count = float(LANES) * jnp.sum(maskv[...].astype(f32), keepdims=True)

    zero = jnp.zeros(shape, f32)
    for it in range(ITERS):
        def magnitudes(e, carry, it=it):
            accs = list(carry)
            if it == 0:
                spec_copy(e).wait()
                east = evp[0, e] - chx[0]
                north = evp[1, e] - chx[1]
                travel = jnp.sqrt(east * east + north * north + evp[2, e] * evp[2, e]) * (1.0 / 3.0)
                level = srcb[e]
            else:
                level = dsb[e]
            for t in range(tiles):
                at = slice(t * LANES, (t + 1) * LANES)
                if it == 0:
                    r = rbuf[e, :, at] - level - site[:, at] + attb * jnp.broadcast_to(travel[t:t + 1, :], shape)
                else:
                    r = rbuf[e, :, at] - level - gath[it - 1, t]
                rbuf[e, :, at] = r
                accs[t % 2] = accs[t % 2] + jnp.abs(r) * mask[e, t].astype(f32)
            return tuple(accs)

        acc = lax.fori_loop(0, n_ev, magnitudes, (zero, zero))
        row = to_row(jnp.sum(acc[0] + acc[1], axis=1, keepdims=True))
        row = jnp.where(lanes[0:1] == freqs, count, row)
        if it == 0:
            pl.semaphore_wait(barrier, len(stage_a) + len(stage_b))
        total = all_sum(it, row)
        number = jnp.sum(jnp.where(lanes[0:1] == freqs, total, 0.0), axis=1, keepdims=True)
        mean = to_column(total) / jnp.maximum(jnp.broadcast_to(number, (freqs, 1)), 1.0)
        limit = jnp.broadcast_to(1.345 * (1.2533 * mean + 1e-05), shape)

        for e in range(n_ev):
            sn[e] = zero
            sd[e] = zero

        def weigh(first, into):
            def pair(j, carry):
                sums = [zero] * 4
                for e in range(n_ev):
                    num = den = None
                    for u in range(2):
                        t = first + 2 * j + u
                        r = rbuf[e, :, pl.ds(pl.multiple_of(t * LANES, LANES), LANES)]
                        w = limit * mask[e, t].astype(f32) / jnp.maximum(jnp.abs(r), limit)
                        p = w * r
                        sums[2 * u] += p
                        sums[2 * u + 1] += w
                        num = p if num is None else num + p
                        den = w if den is None else den + w
                    sn[e] += num
                    sd[e] += den
                for u in range(2):
                    into[2 * j + u, 0] = sums[2 * u]
                    into[2 * j + u, 1] = sums[2 * u + 1]
                return carry
            return pair

        to_sibling = remote(away.at[it], recv_s.at[it], s_send.at[it], s_recv.at[it], sibling)
        lax.fori_loop(0, half // 2, weigh((1 - core) * half, away.at[it]), 0)
        to_sibling.start()
        pending.append(to_sibling)
        lax.fori_loop(0, half // 2, weigh(core * half, own.at[it]), 0)
        to_sibling.wait_recv()
        scatter = []
        for k, g in enumerate(group_chip):
            own[it, g] += recv_s[it, g]
            copy = remote(own.at[it, g], recv_c.at[it, k], c_send.at[it, k], c_recv.at[it, k], group[k])
            copy.start()
            scatter.append(copy)
        pending.extend(scatter)

        packed = zero
        for e in range(n_ev):
            packed = jnp.where(lanes == e, jnp.sum(sn[e], axis=1, keepdims=True), packed)
            packed = jnp.where(lanes == n_ev + e, jnp.sum(sd[e], axis=1, keepdims=True), packed)
        packed = packed[0:8] + pltpu.roll(packed[8:16], 2 * n_ev, axis=1)
        bsend[it] = packed
        along = [
            remote(bsend.at[it], brecv.at[it, k], b_send.at[it, k], b_recv.at[it, k], peer)
            for k, peer in enumerate(chan_peers)
        ]
        for copy in along:
            copy.start()
        pending.extend(along)

        for copy in scatter:
            copy.wait_recv()
        both = own[it, chip] + recv_s[it, chip]
        for k in range(len(group)):
            both = both + recv_c[it, k]
        tile = core * half + chip
        gath[it, tile] = 0.5 * both[0] / (both[1] + 1.0)
        gather = [
            remote(gath.at[it, tile], gath.at[it, tile], g_send.at[it, k], g_recv.at[it, k], peer)
            for k, peer in enumerate(group)
        ]
        if it == ITERS - 1:
            final = site[:, pl.ds(pl.multiple_of(tile * LANES, LANES), LANES)]
            for i in range(ITERS):
                final = final + gath[i, tile]
            last_row = to_row(jnp.sum(final, axis=1, keepdims=True))
        for copy in gather:
            copy.start()
        pending.extend(gather)
        forward = [remote(gath.at[it, tile], gath.at[it, tile], f_send.at[it, 15], f_recv.at[it, 15], sibling)]
        forward[0].start()

        def gather_rest():
            for k, g in enumerate(group_from):
                gather[k].wait_recv()
                come = core * half + g
                copy = remote(gath.at[it, come], gath.at[it, come], f_send.at[it, k], f_recv.at[it, k], sibling)
                copy.start()
                forward.append(copy)
            pending.extend(forward)

        def source_rest():
            for copy in along:
                copy.wait_recv()
            both = bsend[it]
            for k in range(len(chan_peers)):
                both = both + brecv[it, k]
            use = lax.rem(lanes[0:8], 2 * n_ev) < n_ev
            below = jnp.where(use, pltpu.roll(both, LANES - n_ev, axis=1), 0.0)
            step = 0.5 * both / (below + 1.0)
            for e in range(n_ev):
                dsb[e, 0:8] = jnp.broadcast_to(step[:, e:e + 1], (8, LANES))
                dsb[e, 8:16] = jnp.broadcast_to(step[:, 2 * n_ev + e:2 * n_ev + e + 1], (8, LANES))
                srcb[e] += dsb[e]

        if it < ITERS - 1:
            gather_rest()
            source_rest()
            for copy in forward:
                copy.wait_recv()
        else:
            total = all_sum(ITERS, last_row) * (1.0 / (n_ch * Y_HI * Z))
            gather_rest()
            source_rest()
            for copy in forward:
                copy.wait_recv()

    shift = jnp.broadcast_to(to_column(total), shape)
    for t in range(tiles):
        at = slice(t * LANES, (t + 1) * LANES)
        out = site[:, at]
        for i in range(ITERS):
            out = out + gath[i, t]
        site_o[:, at] = out - shift
    for e in range(n_ev):
        out = to_row(srcb[e][:, 0:1]) + total
        source_o[e:e + 1, :] = out[:, 0:freqs]
    for copy in pending:
        copy.wait_send()


def on_device(spectra, tile_mask, source_init, site_init, event_pos, channel_pos, atten):
    n_ev, freqs, n_ch = spectra.shape
    tiles = n_ch // LANES
    half = tiles // 2
    assert half == CHIPS and freqs == n_ev == 16
    v, dma = pltpu.VMEM, pltpu.SemaphoreType.DMA
    ng, na, nb, nc = len(GROUP), len(STAGE_A), len(STAGE_B), len(CHAN)
    block = (freqs, LANES)
    scratch = [
        v((n_ev, freqs, n_ch), f32), v((freqs, n_ch), f32), v((2, n_ch), f32), v((n_ev, freqs), f32),
        v((1, freqs), f32), v((n_ev, tiles), jnp.int32),
        pltpu.SMEM((n_ev, tiles), jnp.int32), pltpu.SMEM((3, n_ev), f32),
        v((2, tiles, LANES), f32), v((n_ev,) + block, f32), v((n_ev,) + block, f32),
        v((n_ev,) + block, f32), v((n_ev,) + block, f32),
        v((ITERS, half, 2) + block, f32), v((ITERS, half, 2) + block, f32), v((ITERS, half, 2) + block, f32),
        v((ITERS, ng, 2) + block, f32), v((ITERS, tiles) + block, f32),
        v((ITERS, 8, LANES), f32), v((ITERS, nc, 8, LANES), f32),
        v((ITERS + 1, 2, 1, LANES), f32), v((ITERS + 1, na, 1, LANES), f32), v((ITERS + 1, nb, 1, LANES), f32),
        dma((n_ev,)), dma((7,)), dma((ITERS,)), dma((ITERS,)),
        dma((ITERS, ng)), dma((ITERS, ng)), dma((ITERS, ng)), dma((ITERS, ng)),
        dma((ITERS, ng + 1)), dma((ITERS, ng + 1)), dma((ITERS, nc)), dma((ITERS, nc)),
        dma((ITERS + 1, na)), dma((ITERS + 1, na)), dma((ITERS + 1, nb)), dma((ITERS + 1, nb)),
    ]
    anywhere = pl.BlockSpec(memory_space=pl.ANY)
    vmem = pl.BlockSpec(memory_space=pltpu.VMEM)
    return pl.pallas_call(
        kernel,
        out_shape=(
            jax.ShapeDtypeStruct((n_ev, freqs), f32),
            jax.ShapeDtypeStruct((freqs, n_ch), f32),
        ),
        in_specs=[anywhere] * 7,
        out_specs=(vmem, vmem),
        scratch_shapes=scratch,
        name="estimate",
        compiler_params=pltpu.CompilerParams(
            collective_id=0, has_side_effects=True, vmem_limit_bytes=40 << 20
        ),
    )(spectra, tile_mask, source_init, site_init, event_pos, channel_pos, atten.reshape(1, freqs))


def solution(mesh):
    in_specs = (
        P("ev", None, "ch"),
        P("ev", "ch"),
        P("ev", None),
        P(None, "ch"),
        P(None, "ev"),
        P(None, "ch"),
        P(),
    )
    out_specs = (P("ev", None), P(None, "ch"))
    return jax.shard_map(
        on_device, mesh=mesh, in_specs=in_specs, out_specs=out_specs, check_vma=False
    )
```

```python
import functools
import jax
import jax.numpy as jnp
from jax import lax
from jax.experimental import pallas as pl
from jax.experimental.pallas import tpu as pltpu
from jax.sharding import PartitionSpec as P

ITERS = 2
LANES = 128
X, Y_LO, CORE, Y_HI, Z = 4, 4, 2, 2, 8
Y = Y_HI * Y_LO
CHIPS = X * Y_LO
f32 = jnp.float32


def ring(step, size):
    return min(step, size - step)


STAGE_A = sorted(
    ((dz, dc) for dz in range(Z) for dc in range(CORE) if dz or dc),
    key=lambda s: -ring(s[0], Z),
)
STAGE_B = sorted(
    ((dy, dx) for dy in range(Y) for dx in range(X) if dy or dx),
    key=lambda s: -ring(s[0], Y) - ring(s[1], X),
)
NEAR = 8


def group_step(p):
    i = p // X
    return (p % X + 1) % X, (2 + i + i * (i - 1) // 2) % Y_LO


def kernel(
    spectra, mask_h, source_h, site_h, event_h, channel_h, atten_h,
    source_o, site_o,
    rbuf, site, chan, srcv, attv, maskv, mask, evp, chx, srcb, dsb, sn, sd, sums,
    away, recv_s, own, recv_x, ysend, recv_y, gath, bsend, brecv, brecv2, arow, arecv_a, arecv_b,
    spec_sem, in_sem, s_send, s_recv, x_send, x_recv, y_send, y_recv, g_send, g_recv, f_send, f_recv,
    b_send, b_recv, a_send, a_recv,
):
    n_ev, freqs, n_ch = rbuf.shape
    tiles = n_ch // LANES
    half = tiles // 2
    part = n_ev // 4
    others = half - 1
    ev, ch = lax.axis_index("ev"), lax.axis_index("ch")
    core, chip = lax.rem(ev, CORE), ev // CORE
    x, y_lo = chip // Y_LO, lax.rem(chip, Y_LO)
    y_hi, z = ch // Z, lax.rem(ch, Z)
    y = y_hi * Y_LO + y_lo

    def place(px, py, pz, pc):
        return ((px * Y_LO + lax.rem(py, Y_LO)) * CORE + pc, (py // Y_LO) * Z + pz)

    stage_a = [place(x, y, lax.rem(z + dz, Z), lax.rem(core + dc, CORE)) for dz, dc in STAGE_A]
    stage_b = [place(lax.rem(x + dx, X), lax.rem(y + dy, Y), z, core) for dy, dx in STAGE_B]
    sibling = (chip * CORE + 1 - core, ch)
    along_z = [(ev, y_hi * Z + lax.rem(z + dz, Z)) for dz in (4, 3, 5, 2, 6, 1, 7)]
    across_y = (ev, (1 - y_hi) * Z + z)

    upper, inner = y_lo // 2, lax.rem((y_lo + 1) // 2, 2)

    def row_of(i):
        there = (1 - upper) * (Y_LO - 1 - i) + upper * i
        return there + i // 2 * inner * (1 - 2 * lax.rem(there, 2))

    across_x = [lax.rem(x + j + 1, X) * Y_LO for j in range(X)]

    def chip_at(p):
        dx, dy = group_step(p)
        return lax.rem(x + dx, X) * Y_LO + lax.rem(y_lo + dy, Y_LO)

    def chip_from(p):
        dx, dy = group_step(p)
        return lax.rem(x + X - dx, X) * Y_LO + lax.rem(y_lo + Y_LO - dy, Y_LO)

    barrier = pltpu.get_barrier_semaphore()
    for peer in stage_b + stage_a:
        pl.semaphore_signal(barrier, inc=1, device_id=peer, device_id_type=pl.DeviceIdType.MESH)

    def remote(src, dst, send, recv, peer):
        return pltpu.make_async_remote_copy(
            src_ref=src, dst_ref=dst, send_sem=send, recv_sem=recv,
            device_id=peer, device_id_type=pl.DeviceIdType.MESH,
        )

    def settle(ref, sem):
        pltpu.make_async_copy(ref, ref, sem).wait()

    def spec_copy(q):
        return pltpu.make_async_copy(spectra.at[pl.ds(q * part, part)], rbuf.at[pl.ds(q * part, part)], spec_sem.at[q])

    small = [
        pltpu.make_async_copy(src, dst, in_sem.at[i])
        for i, (src, dst) in enumerate(
            [(mask_h, mask), (event_h, evp), (channel_h, chan), (atten_h, attv),
             (source_h, srcv), (mask_h, maskv), (site_h, site)]
        )
    ]
    for copy in small:
        copy.start()
    for q in range(n_ev // part):
        spec_copy(q).start()

    shape = (freqs, LANES)
    rows = lax.broadcasted_iota(jnp.int32, shape, 0)
    lanes = lax.broadcasted_iota(jnp.int32, shape, 1)
    diag = rows == lanes

    def to_column(row):
        spread = jnp.where(diag, jnp.broadcast_to(row, shape), 0.0)
        return jnp.sum(spread, axis=1, keepdims=True)

    def to_row(column):
        spread = jnp.where(diag, jnp.broadcast_to(column, shape), 0.0)
        return jnp.sum(spread, axis=0, keepdims=True)

    def tree(parts):
        while len(parts) > 1:
            parts = [a + b for a, b in zip(parts[::2], parts[1::2])] + parts[len(parts) // 2 * 2:]
        return parts[0]

    sent = []

    def all_sum(phase, row, meanwhile=None):
        for stage, peers, landed in ((0, stage_a, arecv_a), (1, stage_b, arecv_b)):
            arow[phase, stage] = row
            for k, peer in enumerate(peers):
                remote(arow.at[phase, stage], landed.at[phase, k], a_send.at[phase, stage], a_recv.at[phase, stage], peer).start()
            sent.append((landed.at[phase], a_send.at[phase, stage]))
            if meanwhile is not None:
                meanwhile[stage]()
            settle(landed.at[phase], a_recv.at[phase, stage])
            row = tree([row] + [landed[phase, k] for k in range(len(peers))])
        return row

    for copy in small[:-1]:
        copy.wait()

    small_shape = (n_ev, freqs)
    small_diag = lax.broadcasted_iota(jnp.int32, small_shape, 0) == lax.broadcasted_iota(jnp.int32, small_shape, 1)

    def widen(row):
        spread = jnp.where(small_diag, jnp.broadcast_to(row, small_shape), 0.0)
        return jnp.broadcast_to(jnp.sum(spread, axis=1, keepdims=True), shape)

    for t in range(tiles):
        chx[0, t:t + 1, :] = chan[0:1, t * LANES:(t + 1) * LANES]
        chx[1, t:t + 1, :] = chan[1:2, t * LANES:(t + 1) * LANES]
    for e in range(n_ev):
        srcb[e] = widen(srcv[e:e + 1, :])
    attb = widen(attv[0:1, :])
    count = float(LANES) * jnp.sum(maskv[...].astype(f32), keepdims=True)

    small[-1].wait()
    zero = jnp.zeros(shape, f32)
    for it in range(ITERS):
        def first(e, carry):
            accs = list(carry)

            @pl.when(lax.rem(e, part) == 0)
            def _():
                spec_copy(e // part).wait()
            east = evp[0, e] - chx[0]
            north = evp[1, e] - chx[1]
            travel = jnp.sqrt(east * east + north * north + evp[2, e] * evp[2, e]) * (1.0 / 3.0)
            for t in range(tiles):
                at = slice(t * LANES, (t + 1) * LANES)
                r = rbuf[e, :, at] - srcb[e] - site[:, at] + attb * jnp.broadcast_to(travel[t:t + 1, :], shape)
                rbuf[e, :, at] = r
                accs[t % 2] = accs[t % 2] + jnp.abs(r) * mask[e, t].astype(f32)
            return tuple(accs)

        def later(side, it=it):
            def update(e, carry):
                accs = list(carry)
                for t in range(side * half, (side + 1) * half):
                    at = slice(t * LANES, (t + 1) * LANES)
                    r = rbuf[e, :, at] - dsb[e] - gath[it - 1, t]
                    rbuf[e, :, at] = r
                    accs[t % 2] = accs[t % 2] + jnp.abs(r) * mask[e, t].astype(f32)
                return tuple(accs)
            return update

        if it == 0:
            first_sum, second_sum = lax.fori_loop(0, n_ev, first, (zero, zero))
            sums[...] = first_sum + second_sum
        else:
            for side in range(CORE):
                @pl.when(core == side)
                def _(side=side, it=it):
                    acc = lax.fori_loop(0, n_ev, later(side), (zero, zero))
                    settle(gath.at[it - 1, pl.ds(0, half)], f_recv.at[it - 1])
                    acc = lax.fori_loop(0, n_ev, later(1 - side), acc)
                    sums[...] = acc[0] + acc[1]
        row = to_row(jnp.sum(sums[...], axis=1, keepdims=True))
        row = jnp.where(lanes[0:1] == freqs, count, row)
        if it == 0:
            pl.semaphore_wait(barrier, len(stage_a) + len(stage_b))
        total = all_sum(it, row)
        number = jnp.sum(jnp.where(lanes[0:1] == freqs, total, 0.0), axis=1, keepdims=True)
        mean = to_column(total) / jnp.maximum(jnp.broadcast_to(number, (freqs, 1)), 1.0)
        limit = jnp.broadcast_to(1.345 * (1.2533 * mean + 1e-05), shape)

        for e in range(n_ev):
            sn[e] = zero
            sd[e] = zero

        def weigh(side, into, i):
            row = row_of(i)
            for j in range(0, X, 2):
                totals = [zero] * 4
                where = [side * half + across_x[j + u] + row for u in range(2)]
                for e in range(n_ev):
                    num = den = None
                    for u, t in enumerate(where):
                        r = rbuf[e, :, pl.ds(pl.multiple_of(t * LANES, LANES), LANES)]
                        w = limit * mask[e, t].astype(f32) / jnp.maximum(jnp.abs(r), limit)
                        p = w * r
                        totals[2 * u] += p
                        totals[2 * u + 1] += w
                        num = p if num is None else num + p
                        den = w if den is None else den + w
                    sn[e] += num
                    sd[e] += den
                for u in range(2):
                    into[X * i + j + u, 0] = totals[2 * u]
                    into[X * i + j + u, 1] = totals[2 * u + 1]

        def give(i, carry):
            weigh(1 - core, away.at[it], i)
            block = pl.ds(X * i, X)
            remote(away.at[it, block], recv_s.at[it, block], s_send.at[it], s_recv.at[it, i], sibling).start()
            return carry

        def take(i, carry):
            weigh(core, own.at[it], i)
            settle(recv_s.at[it, pl.ds(X * i, X)], s_recv.at[it, i])
            for j in (1, 0, 2, 3):
                p = X * i + j
                own[it, p] += recv_s[it, p]
                if j < X - 1:
                    peer = (across_x[j] + y_lo) * CORE + core
                    remote(own.at[it, p], recv_x.at[it, i, j], x_send.at[it], x_recv.at[it, i], (peer, ch)).start()
            return carry

        lax.fori_loop(0, Y_LO, give, 0)
        lax.fori_loop(0, Y_LO, take, 0)
        sent.append((recv_s.at[it], s_send.at[it]))
        sent.append((recv_x.at[it], x_send.at[it]))

        packed = zero
        for e in range(n_ev):
            packed = jnp.where(lanes == e, jnp.sum(sn[e], axis=1, keepdims=True), packed)
            packed = jnp.where(lanes == n_ev + e, jnp.sum(sd[e], axis=1, keepdims=True), packed)
        packed = packed[0:8] + pltpu.roll(packed[8:16], 2 * n_ev, axis=1)
        bsend[it, 0] = packed
        for k, peer in enumerate(along_z):
            remote(bsend.at[it, 0], brecv.at[it, k], b_send.at[it, 0], b_recv.at[it, 0], peer).start()
        sent.append((brecv.at[it], b_send.at[it, 0]))

        for i in range(Y_LO):
            settle(recv_x.at[it, i], x_recv.at[it, i])
            both = tree([own[it, X * i + X - 1]] + [recv_x[it, i, j] for j in range(X - 1)])
            if i < Y_LO - 1:
                ysend[it, i] = both
                slot = lax.rem(row_of(i) + Y_LO - y_lo, Y_LO) - 1
                peer = (x * Y_LO + row_of(i)) * CORE + core
                remote(ysend.at[it, i], recv_y.at[it, slot], y_send.at[it], y_recv.at[it], (peer, ch)).start()
        sent.append((recv_y.at[it], y_send.at[it]))
        settle(recv_y.at[it], y_recv.at[it])
        both = tree([both] + [recv_y[it, i] for i in range(Y_LO - 1)])
        tile = core * half + chip
        gath[it, tile] = 0.5 * both[0] / (both[1] + 1.0)
        if it == ITERS - 1:
            final = site[:, pl.ds(pl.multiple_of(tile * LANES, LANES), LANES)]
            for i in range(ITERS):
                final = final + gath[i, tile]
            last_row = to_row(jnp.sum(final, axis=1, keepdims=True))

        def gather():
            for p in range(others):
                batch = 0 if p < NEAR else 1
                remote(
                    gath.at[it, tile], gath.at[it, tile], g_send.at[it, batch], g_recv.at[it, batch],
                    (chip_at(p) * CORE + core, ch),
                ).start()
            remote(gath.at[it, tile], gath.at[it, tile], f_send.at[it], f_recv.at[it], sibling).start()
            for batch, n in ((0, NEAR), (1, others - NEAR)):
                sent.append((gath.at[it, pl.ds(0, n)], g_send.at[it, batch]))
            sent.append((gath.at[it, pl.ds(0, half)], f_send.at[it]))

        def across():
            settle(brecv.at[it], b_recv.at[it, 0])
            bsend[it, 1] = tree([bsend[it, 0]] + [brecv[it, k] for k in range(len(along_z))])
            remote(bsend.at[it, 1], brecv2.at[it], b_send.at[it, 1], b_recv.at[it, 1], across_y).start()
            sent.append((brecv2.at[it], b_send.at[it, 1]))

        def source_rest():
            settle(brecv2.at[it], b_recv.at[it, 1])
            both = bsend[it, 1] + brecv2[it]
            use = lax.rem(lanes[0:8], 2 * n_ev) < n_ev
            below = jnp.where(use, pltpu.roll(both, LANES - n_ev, axis=1), 0.0)
            step = 0.5 * both / (below + 1.0)
            for e in range(n_ev):
                dsb[e, 0:8] = jnp.broadcast_to(step[:, e:e + 1], (8, LANES))
                dsb[e, 8:16] = jnp.broadcast_to(step[:, 2 * n_ev + e:2 * n_ev + e + 1], (8, LANES))
                srcb[e] += dsb[e]

        def forward():
            for batch, (first, last) in enumerate(((0, NEAR), (NEAR, others))):
                settle(gath.at[it, pl.ds(0, last - first)], g_recv.at[it, batch])
                for p in range(first, last):
                    come = core * half + chip_from(p)
                    remote(gath.at[it, come], gath.at[it, come], f_send.at[it], f_recv.at[it], sibling).start()

        if it < ITERS - 1:
            gather()
            across()
            forward()
            source_rest()
        else:
            def meanwhile():
                across()
                forward()
            total = all_sum(ITERS, last_row, (gather, meanwhile)) * (1.0 / (n_ch * Y_HI * Z))
            source_rest()
            settle(gath.at[it, pl.ds(0, half)], f_recv.at[it])

    shift = jnp.broadcast_to(to_column(total), shape)
    for t in range(tiles):
        at = slice(t * LANES, (t + 1) * LANES)
        out = site[:, at]
        for i in range(ITERS):
            out = out + gath[i, t]
        site_o[:, at] = out - shift
    for e in range(n_ev):
        out = to_row(srcb[e][:, 0:1]) + total
        source_o[e:e + 1, :] = out[:, 0:freqs]
    for ref, sem in sent:
        settle(ref, sem)


def on_device(spectra, tile_mask, source_init, site_init, event_pos, channel_pos, atten):
    n_ev, freqs, n_ch = spectra.shape
    tiles = n_ch // LANES
    half = tiles // 2
    assert half == CHIPS and freqs == n_ev == 16
    v, dma = pltpu.VMEM, pltpu.SemaphoreType.DMA
    na, nb = len(STAGE_A), len(STAGE_B)
    block = (freqs, LANES)
    scratch = [
        v((n_ev, freqs, n_ch), f32), v((freqs, n_ch), f32), v((2, n_ch), f32), v((n_ev, freqs), f32),
        v((1, freqs), f32), v((n_ev, tiles), jnp.int32),
        pltpu.SMEM((n_ev, tiles), jnp.int32), pltpu.SMEM((3, n_ev), f32),
        v((2, tiles, LANES), f32), v((n_ev,) + block, f32), v((n_ev,) + block, f32),
        v((n_ev,) + block, f32), v((n_ev,) + block, f32), v(block, f32),
        v((ITERS, half, 2) + block, f32), v((ITERS, half, 2) + block, f32), v((ITERS, half, 2) + block, f32),
        v((ITERS, Y_LO, X - 1, 2) + block, f32), v((ITERS, Y_LO - 1, 2) + block, f32), v((ITERS, Y_LO - 1, 2) + block, f32),
        v((ITERS, tiles) + block, f32),
        v((ITERS, 2, 8, LANES), f32), v((ITERS, Z - 1, 8, LANES), f32), v((ITERS, 8, LANES), f32),
        v((ITERS + 1, 2, 1, LANES), f32), v((ITERS + 1, na, 1, LANES), f32), v((ITERS + 1, nb, 1, LANES), f32),
        dma((4,)), dma((7,)), dma((ITERS,)), dma((ITERS, Y_LO)), dma((ITERS,)), dma((ITERS, Y_LO)), dma((ITERS,)), dma((ITERS,)),
        dma((ITERS, 2)), dma((ITERS, 2)), dma((ITERS,)), dma((ITERS,)),
        dma((ITERS, 2)), dma((ITERS, 2)), dma((ITERS + 1, 2)), dma((ITERS + 1, 2)),
    ]
    hbm = pl.BlockSpec(memory_space=pltpu.HBM)
    vmem = pl.BlockSpec(memory_space=pltpu.VMEM)
    shapes = (jax.ShapeDtypeStruct((n_ev, freqs), f32), jax.ShapeDtypeStruct((freqs, n_ch), f32))
    inputs = (spectra, tile_mask, source_init, site_init, event_pos, channel_pos, atten.reshape(1, freqs))
    return pl.pallas_call(
        kernel,
        out_shape=shapes,
        in_specs=[hbm] * len(inputs),
        out_specs=(vmem, vmem),
        scratch_shapes=scratch,
        name="estimate",
        compiler_params=pltpu.CompilerParams(
            collective_id=0, has_side_effects=True, vmem_limit_bytes=40 << 20
        ),
    )(*[pltpu.with_memory_space_constraint(v, pltpu.HBM) for v in inputs])


def solution(mesh):
    in_specs = (
        P("ev", None, "ch"),
        P("ev", "ch"),
        P("ev", None),
        P(None, "ch"),
        P(None, "ev"),
        P(None, "ch"),
        P(),
    )
    out_specs = (P("ev", None), P(None, "ch"))
    return jax.shard_map(
        on_device, mesh=mesh, in_specs=in_specs, out_specs=out_specs, check_vma=False
    )
```

```python
import functools
import jax
import jax.numpy as jnp
from jax import lax
from jax.experimental import pallas as pl
from jax.experimental.pallas import tpu as pltpu
from jax.sharding import PartitionSpec as P

ITERS = 2
LANES = 128
X, Y_LO, CORE, Y_HI, Z = 4, 4, 2, 2, 8
Y = Y_HI * Y_LO
CHIPS = X * Y_LO
f32 = jnp.float32


def ring(step, size):
    return min(step, size - step)


STAGE_A = sorted(
    ((dz, dc) for dz in range(Z) for dc in range(CORE) if dz or dc),
    key=lambda s: -ring(s[0], Z),
)
STAGE_B = sorted(
    ((dy, dx) for dy in range(Y) for dx in range(X) if dy or dx),
    key=lambda s: -ring(s[0], Y) - ring(s[1], X),
)
EVERYONE = sorted(
    ((dx, dy, dz) for dx in range(X) for dy in range(Y) for dz in range(Z) if dx or dy or dz),
    key=lambda s: -ring(s[0], X) - ring(s[1], Y) - ring(s[2], Z),
)
NEAR = 8


def group_step(p):
    i = p // X
    return (p % X + 1) % X, (2 + i + i * (i - 1) // 2) % Y_LO


def kernel(
    spectra, mask_h, source_h, site_h, event_h, channel_h, atten_h,
    source_o, site_o,
    rbuf, site, chan, srcv, attv, maskv, mask, evp, chx, srcb, dsb, sn, sd, sums,
    away, recv_s, own, recv_x, ysend, recv_y, gath, bsend, brecv, brecv2, arow, arecv_a, arecv_b, arecv_all,
    spec_sem, in_sem, s_send, s_recv, x_send, x_recv, y_send, y_recv, g_send, g_recv, f_send, f_recv,
    b_send, b_recv, a_send, a_recv, all_send, all_recv,
):
    n_ev, freqs, n_ch = rbuf.shape
    tiles = n_ch // LANES
    half = tiles // 2
    part = n_ev // 4
    others = half - 1
    ev, ch = lax.axis_index("ev"), lax.axis_index("ch")
    core, chip = lax.rem(ev, CORE), ev // CORE
    x, y_lo = chip // Y_LO, lax.rem(chip, Y_LO)
    y_hi, z = ch // Z, lax.rem(ch, Z)
    y = y_hi * Y_LO + y_lo

    def place(px, py, pz, pc):
        return ((px * Y_LO + lax.rem(py, Y_LO)) * CORE + pc, (py // Y_LO) * Z + pz)

    stage_a = [place(x, y, lax.rem(z + dz, Z), lax.rem(core + dc, CORE)) for dz, dc in STAGE_A]
    stage_b = [place(lax.rem(x + dx, X), lax.rem(y + dy, Y), z, core) for dy, dx in STAGE_B]
    sibling = (chip * CORE + 1 - core, ch)
    along_z = [(ev, y_hi * Z + lax.rem(z + dz, Z)) for dz in (4, 3, 5, 2, 6, 1, 7)]
    across_y = (ev, (1 - y_hi) * Z + z)

    upper, inner = y_lo // 2, lax.rem((y_lo + 1) // 2, 2)

    def row_of(i):
        there = (1 - upper) * (Y_LO - 1 - i) + upper * i
        return there + i // 2 * inner * (1 - 2 * lax.rem(there, 2))

    across_x = [lax.rem(x + j + 1, X) * Y_LO for j in range(X)]

    def chip_at(p):
        dx, dy = group_step(p)
        return lax.rem(x + dx, X) * Y_LO + lax.rem(y_lo + dy, Y_LO)

    def chip_from(p):
        dx, dy = group_step(p)
        return lax.rem(x + X - dx, X) * Y_LO + lax.rem(y_lo + Y_LO - dy, Y_LO)

    barrier = pltpu.get_barrier_semaphore()
    for peer in stage_b + stage_a:
        pl.semaphore_signal(barrier, inc=1, device_id=peer, device_id_type=pl.DeviceIdType.MESH)

    def remote(src, dst, send, recv, peer):
        return pltpu.make_async_remote_copy(
            src_ref=src, dst_ref=dst, send_sem=send, recv_sem=recv,
            device_id=peer, device_id_type=pl.DeviceIdType.MESH,
        )

    def settle(ref, sem):
        pltpu.make_async_copy(ref, ref, sem).wait()

    def spec_copy(q):
        return pltpu.make_async_copy(spectra.at[pl.ds(q * part, part)], rbuf.at[pl.ds(q * part, part)], spec_sem.at[q])

    small = [
        pltpu.make_async_copy(src, dst, in_sem.at[i])
        for i, (src, dst) in enumerate(
            [(mask_h, mask), (event_h, evp), (channel_h, chan), (atten_h, attv),
             (source_h, srcv), (mask_h, maskv), (site_h, site)]
        )
    ]
    for copy in small:
        copy.start()
    for q in range(n_ev // part):
        spec_copy(q).start()

    shape = (freqs, LANES)
    rows = lax.broadcasted_iota(jnp.int32, shape, 0)
    lanes = lax.broadcasted_iota(jnp.int32, shape, 1)
    diag = rows == lanes

    def to_column(row):
        spread = jnp.where(diag, jnp.broadcast_to(row, shape), 0.0)
        return jnp.sum(spread, axis=1, keepdims=True)

    def to_row(column):
        spread = jnp.where(diag, jnp.broadcast_to(column, shape), 0.0)
        return jnp.sum(spread, axis=0, keepdims=True)

    def tree(parts):
        while len(parts) > 1:
            parts = [a + b for a, b in zip(parts[::2], parts[1::2])] + parts[len(parts) // 2 * 2:]
        return parts[0]

    sent = []

    def drain():
        for ref, sem in sent:
            settle(ref, sem)
        sent.clear()

    def all_sum(turn, row, after_first=None, after_second=None):
        for stage, peers, landed in ((0, stage_a, arecv_a), (1, stage_b, arecv_b)):
            arow[turn, stage] = row
            for k, peer in enumerate(peers):
                remote(arow.at[turn, stage], landed.at[turn, k], a_send.at[turn, stage], a_recv.at[turn, stage], peer).start()
            sent.append((landed.at[turn], a_send.at[turn, stage]))
            after = (after_first, after_second)[stage]
            if after is not None:
                after()
            settle(landed.at[turn], a_recv.at[turn, stage])
            row = tree([row] + [landed[turn, k] for k in range(len(peers))])
        return row

    xs = [lax.rem(x + dx, X) for dx in range(X)]
    ys = [lax.rem(y + dy, Y) for dy in range(Y)]
    zs = [lax.rem(z + dz, Z) for dz in range(Z)]
    ev_at = [[(px * Y_LO + lax.rem(py, Y_LO)) * CORE + core for py in ys] for px in xs]
    ch_at = [[(py // Y_LO) * Z + pz for pz in zs] for py in ys]

    def all_sum_direct(row):
        arow[1, 0] = row
        pair, landed = arecv_all.at[pl.ds(len(EVERYONE), 1)], arecv_all.at[pl.ds(0, len(EVERYONE))]
        remote(arow.at[1, pl.ds(0, 1)], pair, all_send.at[0], all_recv.at[0], sibling).start()
        settle(pair, all_recv.at[0])
        row = row + arecv_all[len(EVERYONE)]
        arow[1, 1] = row
        for k, (dx, dy, dz) in enumerate(EVERYONE):
            remote(arow.at[1, 1], arecv_all.at[k], all_send.at[1], all_recv.at[1], (ev_at[dx][dy], ch_at[dy][dz])).start()
        sent.append((pair, all_send.at[0]))
        sent.append((landed, all_send.at[1]))
        settle(landed, all_recv.at[1])
        return tree([row] + [arecv_all[k] for k in range(len(EVERYONE))])

    for copy in small[:-1]:
        copy.wait()

    small_shape = (n_ev, freqs)
    small_diag = lax.broadcasted_iota(jnp.int32, small_shape, 0) == lax.broadcasted_iota(jnp.int32, small_shape, 1)

    def widen(row):
        spread = jnp.where(small_diag, jnp.broadcast_to(row, small_shape), 0.0)
        return jnp.broadcast_to(jnp.sum(spread, axis=1, keepdims=True), shape)

    for t in range(tiles):
        chx[0, t:t + 1, :] = chan[0:1, t * LANES:(t + 1) * LANES]
        chx[1, t:t + 1, :] = chan[1:2, t * LANES:(t + 1) * LANES]
    for e in range(n_ev):
        srcb[e] = widen(srcv[e:e + 1, :])
    attb = widen(attv[0:1, :])
    count = float(LANES) * jnp.sum(maskv[...].astype(f32), keepdims=True)

    small[-1].wait()
    zero = jnp.zeros(shape, f32)
    for it in range(ITERS):
        def first(e, carry):
            accs = list(carry)

            @pl.when(lax.rem(e, part) == 0)
            def _():
                spec_copy(e // part).wait()
            east = evp[0, e] - chx[0]
            north = evp[1, e] - chx[1]
            travel = jnp.sqrt(east * east + north * north + evp[2, e] * evp[2, e]) * (1.0 / 3.0)
            for t in range(tiles):
                at = slice(t * LANES, (t + 1) * LANES)
                r = rbuf[e, :, at] - srcb[e] - site[:, at] + attb * jnp.broadcast_to(travel[t:t + 1, :], shape)
                rbuf[e, :, at] = r
                accs[t % 2] = accs[t % 2] + jnp.abs(r) * mask[e, t].astype(f32)
            return tuple(accs)

        def later(side, it=it):
            def update(e, carry):
                accs = list(carry)
                for t in range(side * half, (side + 1) * half):
                    at = slice(t * LANES, (t + 1) * LANES)
                    r = rbuf[e, :, at] - dsb[e] - gath[it - 1, t]
                    rbuf[e, :, at] = r
                    accs[t % 2] = accs[t % 2] + jnp.abs(r) * mask[e, t].astype(f32)
                return tuple(accs)
            return update

        if it == 0:
            first_sum, second_sum = lax.fori_loop(0, n_ev, first, (zero, zero))
            sums[...] = first_sum + second_sum
        else:
            for side in range(CORE):
                @pl.when(core == side)
                def _(side=side, it=it):
                    acc = lax.fori_loop(0, n_ev, later(side), (zero, zero))
                    settle(gath.at[it - 1, pl.ds(0, half)], f_recv.at[0])
                    acc = lax.fori_loop(0, n_ev, later(1 - side), acc)
                    sums[...] = acc[0] + acc[1]
        row = to_row(jnp.sum(sums[...], axis=1, keepdims=True))
        row = jnp.where(lanes[0:1] == freqs, count, row)
        drain()
        if it == 0:
            pl.semaphore_wait(barrier, len(stage_a) + len(stage_b))
        total = all_sum(0, row) if it == 0 else all_sum_direct(row)
        number = jnp.sum(jnp.where(lanes[0:1] == freqs, total, 0.0), axis=1, keepdims=True)
        mean = to_column(total) / jnp.maximum(jnp.broadcast_to(number, (freqs, 1)), 1.0)
        limit = jnp.broadcast_to(1.345 * (1.2533 * mean + 1e-05), shape)

        for e in range(n_ev):
            sn[e] = zero
            sd[e] = zero

        def weigh(side, into, i):
            row = row_of(i)
            for j in range(0, X, 2):
                totals = [zero] * 4
                where = [side * half + across_x[j + u] + row for u in range(2)]
                for e in range(n_ev):
                    num = den = None
                    for u, t in enumerate(where):
                        r = rbuf[e, :, pl.ds(pl.multiple_of(t * LANES, LANES), LANES)]
                        w = limit * mask[e, t].astype(f32) / jnp.maximum(jnp.abs(r), limit)
                        p = w * r
                        totals[2 * u] += p
                        totals[2 * u + 1] += w
                        num = p if num is None else num + p
                        den = w if den is None else den + w
                    sn[e] += num
                    sd[e] += den
                for u in range(2):
                    into[X * i + j + u, 0] = totals[2 * u]
                    into[X * i + j + u, 1] = totals[2 * u + 1]

        def give(i, carry):
            weigh(1 - core, away.at[it], i)
            block = pl.ds(X * i, X)
            remote(away.at[it, block], recv_s.at[it, block], s_send.at[0], s_recv.at[i], sibling).start()
            return carry

        def take(i, carry):
            weigh(core, own.at[it], i)
            settle(recv_s.at[it, pl.ds(X * i, X)], s_recv.at[i])
            for j in (1, 0, 2, 3):
                p = X * i + j
                own[it, p] += recv_s[it, p]
                if j < X - 1:
                    peer = (across_x[j] + y_lo) * CORE + core
                    remote(own.at[it, p], recv_x.at[it, i, j], x_send.at[0], x_recv.at[i], (peer, ch)).start()
            return carry

        lax.fori_loop(0, Y_LO, give, 0)
        lax.fori_loop(0, Y_LO, take, 0)
        sent.append((recv_s.at[it], s_send.at[0]))
        sent.append((recv_x.at[it], x_send.at[0]))

        packed = zero
        for e in range(n_ev):
            packed = jnp.where(lanes == e, jnp.sum(sn[e], axis=1, keepdims=True), packed)
            packed = jnp.where(lanes == n_ev + e, jnp.sum(sd[e], axis=1, keepdims=True), packed)
        packed = packed[0:8] + pltpu.roll(packed[8:16], 2 * n_ev, axis=1)
        bsend[it, 0] = packed
        for k, peer in enumerate(along_z):
            remote(bsend.at[it, 0], brecv.at[it, k], b_send.at[0], b_recv.at[0], peer).start()
        sent.append((brecv.at[it], b_send.at[0]))

        for i in range(Y_LO):
            settle(recv_x.at[it, i], x_recv.at[i])
            both = tree([own[it, X * i + X - 1]] + [recv_x[it, i, j] for j in range(X - 1)])
            if i < Y_LO - 1:
                ysend[it, i] = both
                slot = lax.rem(row_of(i) + Y_LO - y_lo, Y_LO) - 1
                peer = (x * Y_LO + row_of(i)) * CORE + core
                remote(ysend.at[it, i], recv_y.at[it, slot], y_send.at[0], y_recv.at[0], (peer, ch)).start()
        sent.append((recv_y.at[it], y_send.at[0]))
        settle(recv_y.at[it], y_recv.at[0])
        both = tree([both] + [recv_y[it, i] for i in range(Y_LO - 1)])
        tile = core * half + chip
        gath[it, tile] = 0.5 * both[0] / (both[1] + 1.0)
        if it == ITERS - 1:
            final = site[:, pl.ds(pl.multiple_of(tile * LANES, LANES), LANES)]
            for i in range(ITERS):
                final = final + gath[i, tile]
            last_row = to_row(jnp.sum(final, axis=1, keepdims=True))

        def gather():
            for p in range(others):
                batch = 0 if p < NEAR else 1
                remote(
                    gath.at[it, tile], gath.at[it, tile], g_send.at[0], g_recv.at[batch],
                    (chip_at(p) * CORE + core, ch),
                ).start()
            remote(gath.at[it, tile], gath.at[it, tile], f_send.at[0], f_recv.at[0], sibling).start()
            sent.append((gath.at[it, pl.ds(0, others)], g_send.at[0]))
            sent.append((gath.at[it, pl.ds(0, half)], f_send.at[0]))

        def across():
            settle(brecv.at[it], b_recv.at[0])
            bsend[it, 1] = tree([bsend[it, 0]] + [brecv[it, k] for k in range(len(along_z))])
            remote(bsend.at[it, 1], brecv2.at[it], b_send.at[1], b_recv.at[1], across_y).start()
            sent.append((brecv2.at[it], b_send.at[1]))

        def source_rest():
            settle(brecv2.at[it], b_recv.at[1])
            both = bsend[it, 1] + brecv2[it]
            use = lax.rem(lanes[0:8], 2 * n_ev) < n_ev
            below = jnp.where(use, pltpu.roll(both, LANES - n_ev, axis=1), 0.0)
            step = 0.5 * both / (below + 1.0)
            for e in range(n_ev):
                dsb[e, 0:8] = jnp.broadcast_to(step[:, e:e + 1], (8, LANES))
                dsb[e, 8:16] = jnp.broadcast_to(step[:, 2 * n_ev + e:2 * n_ev + e + 1], (8, LANES))
                srcb[e] += dsb[e]

        def forward():
            for batch, (first, last) in enumerate(((0, NEAR), (NEAR, others))):
                settle(gath.at[it, pl.ds(0, last - first)], g_recv.at[batch])
                for p in range(first, last):
                    come = core * half + chip_from(p)
                    remote(gath.at[it, come], gath.at[it, come], f_send.at[0], f_recv.at[0], sibling).start()

        if it < ITERS - 1:
            gather()
            across()
            forward()
            source_rest()
        else:
            def meanwhile():
                across()
                forward()
            total = all_sum(2, last_row, gather, meanwhile) * (1.0 / (n_ch * Y_HI * Z))
            source_rest()
            settle(gath.at[it, pl.ds(0, half)], f_recv.at[0])

    shift = jnp.broadcast_to(to_column(total), shape)
    for t in range(tiles):
        at = slice(t * LANES, (t + 1) * LANES)
        out = site[:, at]
        for i in range(ITERS):
            out = out + gath[i, t]
        site_o[:, at] = out - shift
    for e in range(n_ev):
        out = to_row(srcb[e][:, 0:1]) + total
        source_o[e:e + 1, :] = out[:, 0:freqs]
    drain()


def store(source, site, source_o, site_o, sem):
    copies = [
        pltpu.make_async_copy(src, dst, sem.at[i]) for i, (src, dst) in enumerate(((source, source_o), (site, site_o)))
    ]
    for copy in copies:
        copy.start()
    for copy in copies:
        copy.wait()


def on_device(spectra, tile_mask, source_init, site_init, event_pos, channel_pos, atten):
    n_ev, freqs, n_ch = spectra.shape
    tiles = n_ch // LANES
    half = tiles // 2
    assert half == CHIPS and freqs == n_ev == 16
    v, dma = pltpu.VMEM, pltpu.SemaphoreType.DMA
    na, nb = len(STAGE_A), len(STAGE_B)
    block = (freqs, LANES)
    scratch = [
        v((n_ev, freqs, n_ch), f32), v((freqs, n_ch), f32), v((2, n_ch), f32), v((n_ev, freqs), f32),
        v((1, freqs), f32), v((n_ev, tiles), jnp.int32),
        pltpu.SMEM((n_ev, tiles), jnp.int32), pltpu.SMEM((3, n_ev), f32),
        v((2, tiles, LANES), f32), v((n_ev,) + block, f32), v((n_ev,) + block, f32),
        v((n_ev,) + block, f32), v((n_ev,) + block, f32), v(block, f32),
        v((ITERS, half, 2) + block, f32), v((ITERS, half, 2) + block, f32), v((ITERS, half, 2) + block, f32),
        v((ITERS, Y_LO, X - 1, 2) + block, f32), v((ITERS, Y_LO - 1, 2) + block, f32), v((ITERS, Y_LO - 1, 2) + block, f32),
        v((ITERS, tiles) + block, f32),
        v((ITERS, 2, 8, LANES), f32), v((ITERS, Z - 1, 8, LANES), f32), v((ITERS, 8, LANES), f32),
        v((ITERS + 1, 2, 1, LANES), f32), v((ITERS + 1, na, 1, LANES), f32), v((ITERS + 1, nb, 1, LANES), f32),
        v((len(EVERYONE) + 1, 1, LANES), f32),
        dma((4,)), dma((7,)), dma((1,)), dma((Y_LO,)), dma((1,)), dma((Y_LO,)), dma((1,)), dma((1,)),
        dma((1,)), dma((2,)), dma((1,)), dma((1,)), dma((2,)), dma((2,)), dma((ITERS + 1, 2)), dma((ITERS + 1, 2)), dma((2,)), dma((2,)),
    ]
    hbm = pl.BlockSpec(memory_space=pltpu.HBM)
    vmem = pl.BlockSpec(memory_space=pltpu.VMEM)
    shapes = (jax.ShapeDtypeStruct((n_ev, freqs), f32), jax.ShapeDtypeStruct((freqs, n_ch), f32))
    inputs = (spectra, tile_mask, source_init, site_init, event_pos, channel_pos, atten.reshape(1, freqs))
    results = pl.pallas_call(
        kernel,
        out_shape=tuple(pltpu.VMEM(v.shape, f32) for v in shapes),
        in_specs=[hbm] * len(inputs),
        out_specs=(vmem, vmem),
        scratch_shapes=scratch,
        name="estimate",
        compiler_params=pltpu.CompilerParams(
            collective_id=0, has_side_effects=True, vmem_limit_bytes=40 << 20
        ),
    )(*[pltpu.with_memory_space_constraint(v, pltpu.HBM) for v in inputs])
    return pl.pallas_call(
        store,
        out_shape=shapes,
        in_specs=[vmem, vmem],
        out_specs=(hbm, hbm),
        scratch_shapes=[dma((2,))],
        name="store",
    )(*[pltpu.with_memory_space_constraint(v, pltpu.VMEM) for v in results])


def solution(mesh):
    in_specs = (
        P("ev", None, "ch"),
        P("ev", "ch"),
        P("ev", None),
        P(None, "ch"),
        P(None, "ev"),
        P(None, "ch"),
        P(),
    )
    out_specs = (P("ev", None), P(None, "ch"))
    return jax.shard_map(
        on_device, mesh=mesh, in_specs=in_specs, out_specs=out_specs, check_vma=False
    )
```

```python
import functools
import jax
import jax.numpy as jnp
from jax import lax
from jax.experimental import pallas as pl
from jax.experimental.pallas import tpu as pltpu
from jax.sharding import PartitionSpec as P

ITERS = 2
LANES = 128
X, Y_LO, CORE, Y_HI, Z = 4, 4, 2, 2, 8
Y = Y_HI * Y_LO
CHIPS = X * Y_LO
f32 = jnp.float32


def ring(step, size):
    return min(step, size - step)


STAGE_A = sorted(
    ((dz, dc) for dz in range(Z) for dc in range(CORE) if dz or dc),
    key=lambda s: -ring(s[0], Z),
)
STAGE_B = sorted(
    ((dy, dx) for dy in range(Y) for dx in range(X) if dy or dx),
    key=lambda s: -ring(s[0], Y) - ring(s[1], X),
)
EVERYONE = sorted(
    ((dx, dy, dz) for dx in range(X) for dy in range(Y) for dz in range(Z) if dx or dy or dz),
    key=lambda s: -ring(s[0], X) - ring(s[1], Y) - ring(s[2], Z),
)
NEAR = 8


def group_step(p):
    i = p // X
    return (p % X + 1) % X, (2 + i + i * (i - 1) // 2) % Y_LO


def kernel(
    spectra, mask_h, source_h, site_h, event_h, channel_h, atten_h,
    source_o, site_o,
    rbuf, site, chan, srcv, attv, maskv, mask, evp, chx, srcb, dsb, sn, sd, sums,
    away, recv_s, own, recv_x, ysend, recv_y, gath, bsend, brecv, brecv2, arow, arecv_p, arecv_a, arecv_b, arecv_all,
    spec_sem, in_sem, s_send, s_recv, x_send, x_recv, y_send, y_recv, g_send, g_recv, f_send, f_recv,
    b_send, b_recv, a_send, a_recv, all_send, all_recv,
):
    n_ev, freqs, n_ch = rbuf.shape
    tiles = n_ch // LANES
    half = tiles // 2
    part = n_ev // 4
    others = half - 1
    ev, ch = lax.axis_index("ev"), lax.axis_index("ch")
    core, chip = lax.rem(ev, CORE), ev // CORE
    x, y_lo = chip // Y_LO, lax.rem(chip, Y_LO)
    y_hi, z = ch // Z, lax.rem(ch, Z)
    y = y_hi * Y_LO + y_lo

    def place(px, py, pz, pc):
        return ((px * Y_LO + lax.rem(py, Y_LO)) * CORE + pc, (py // Y_LO) * Z + pz)

    stage_a = [place(x, y, lax.rem(z + dz, Z), lax.rem(core + dc, CORE)) for dz, dc in STAGE_A]
    stage_b = [place(lax.rem(x + dx, X), lax.rem(y + dy, Y), z, core) for dy, dx in STAGE_B]
    sibling = (chip * CORE + 1 - core, ch)
    along_z = [(ev, y_hi * Z + lax.rem(z + dz, Z)) for dz in (4, 3, 5, 2, 6, 1, 7)]
    across_y = (ev, (1 - y_hi) * Z + z)

    upper, inner = y_lo // 2, lax.rem((y_lo + 1) // 2, 2)

    def row_of(i):
        there = (1 - upper) * (Y_LO - 1 - i) + upper * i
        return there + i // 2 * inner * (1 - 2 * lax.rem(there, 2))

    across_x = [lax.rem(x + j + 1, X) * Y_LO for j in range(X)]

    def chip_at(p):
        dx, dy = group_step(p)
        return lax.rem(x + dx, X) * Y_LO + lax.rem(y_lo + dy, Y_LO)

    def chip_from(p):
        dx, dy = group_step(p)
        return lax.rem(x + X - dx, X) * Y_LO + lax.rem(y_lo + Y_LO - dy, Y_LO)

    barrier = pltpu.get_barrier_semaphore()
    greeted = stage_b + stage_a
    for peer in greeted:
        pl.semaphore_signal(barrier, inc=1, device_id=peer, device_id_type=pl.DeviceIdType.MESH)

    def remote(src, dst, send, recv, peer):
        return pltpu.make_async_remote_copy(
            src_ref=src, dst_ref=dst, send_sem=send, recv_sem=recv,
            device_id=peer, device_id_type=pl.DeviceIdType.MESH,
        )

    def settle(ref, sem):
        pltpu.make_async_copy(ref, ref, sem).wait()

    def spec_copy(q):
        return pltpu.make_async_copy(spectra.at[pl.ds(q * part, part)], rbuf.at[pl.ds(q * part, part)], spec_sem.at[q])

    small = [
        pltpu.make_async_copy(src, dst, in_sem.at[i])
        for i, (src, dst) in enumerate(
            [(mask_h, mask), (event_h, evp), (channel_h, chan), (atten_h, attv),
             (source_h, srcv), (mask_h, maskv), (site_h, site)]
        )
    ]
    for copy in small:
        copy.start()
    for q in range(n_ev // part):
        spec_copy(q).start()

    shape = (freqs, LANES)
    rows = lax.broadcasted_iota(jnp.int32, shape, 0)
    lanes = lax.broadcasted_iota(jnp.int32, shape, 1)
    diag = rows == lanes

    def to_column(row):
        spread = jnp.where(diag, jnp.broadcast_to(row, shape), 0.0)
        return jnp.sum(spread, axis=1, keepdims=True)

    def to_row(column):
        spread = jnp.where(diag, jnp.broadcast_to(column, shape), 0.0)
        return jnp.sum(spread, axis=0, keepdims=True)

    def tree(parts):
        while len(parts) > 1:
            parts = [a + b for a, b in zip(parts[::2], parts[1::2])] + parts[len(parts) // 2 * 2:]
        return parts[0]

    sent = []

    def drain():
        for ref, sem in sent:
            settle(ref, sem)
        sent.clear()

    def all_sum(turn, stages, row):
        for stage, (peers, landed, after) in enumerate(stages):
            arow[turn, stage] = row
            for k, peer in enumerate(peers):
                remote(arow.at[turn, stage], landed.at[k], a_send.at[turn, stage], a_recv.at[turn, stage], peer).start()
            sent.append((landed, a_send.at[turn, stage]))
            if after is not None:
                after()
            settle(landed, a_recv.at[turn, stage])
            row = tree([row] + [landed[k] for k in range(len(peers))])
        return row

    xs = [lax.rem(x + dx, X) for dx in range(X)]
    ys = [lax.rem(y + dy, Y) for dy in range(Y)]
    zs = [lax.rem(z + dz, Z) for dz in range(Z)]
    ev_at = [[(px * Y_LO + lax.rem(py, Y_LO)) * CORE + core for py in ys] for px in xs]
    ch_at = [[(py // Y_LO) * Z + pz for pz in zs] for py in ys]

    def all_sum_direct(row):
        row = all_sum(1, [([sibling], arecv_p, drain)], row)
        landed = arecv_all
        arow[1, 1] = row
        for k, (dx, dy, dz) in enumerate(EVERYONE):
            remote(arow.at[1, 1], arecv_all.at[k], all_send.at[0], all_recv.at[0], (ev_at[dx][dy], ch_at[dy][dz])).start()
        sent.append((landed, all_send.at[0]))
        settle(landed, all_recv.at[0])
        return tree([row] + [arecv_all[k] for k in range(len(EVERYONE))])

    for copy in small[:-1]:
        copy.wait()

    small_shape = (n_ev, freqs)
    small_diag = lax.broadcasted_iota(jnp.int32, small_shape, 0) == lax.broadcasted_iota(jnp.int32, small_shape, 1)

    def widen(row):
        spread = jnp.where(small_diag, jnp.broadcast_to(row, small_shape), 0.0)
        return jnp.broadcast_to(jnp.sum(spread, axis=1, keepdims=True), shape)

    for t in range(tiles):
        chx[0, t:t + 1, :] = chan[0:1, t * LANES:(t + 1) * LANES]
        chx[1, t:t + 1, :] = chan[1:2, t * LANES:(t + 1) * LANES]
    for e in range(n_ev):
        srcb[e] = widen(srcv[e:e + 1, :])
    attb = widen(attv[0:1, :])
    count = float(LANES) * jnp.sum(maskv[...].astype(f32), keepdims=True)

    small[-1].wait()
    zero = jnp.zeros(shape, f32)
    for it in range(ITERS):
        def first(e, carry):
            accs = list(carry)

            @pl.when(lax.rem(e, part) == 0)
            def _():
                spec_copy(e // part).wait()
            east = evp[0, e] - chx[0]
            north = evp[1, e] - chx[1]
            travel = jnp.sqrt(east * east + north * north + evp[2, e] * evp[2, e]) * (1.0 / 3.0)
            for t in range(tiles):
                at = slice(t * LANES, (t + 1) * LANES)
                r = rbuf[e, :, at] - srcb[e] - site[:, at] + attb * jnp.broadcast_to(travel[t:t + 1, :], shape)
                rbuf[e, :, at] = r
                accs[t % 2] = accs[t % 2] + jnp.abs(r) * mask[e, t].astype(f32)
            return tuple(accs)

        def later(side, it=it):
            def update(e, carry):
                accs = list(carry)
                for t in range(side * half, (side + 1) * half):
                    at = slice(t * LANES, (t + 1) * LANES)
                    r = rbuf[e, :, at] - dsb[e] - gath[it - 1, t]
                    rbuf[e, :, at] = r
                    accs[t % 2] = accs[t % 2] + jnp.abs(r) * mask[e, t].astype(f32)
                return tuple(accs)
            return update

        if it == 0:
            first_sum, second_sum = lax.fori_loop(0, n_ev, first, (zero, zero))
            sums[...] = first_sum + second_sum
        else:
            for side in range(CORE):
                @pl.when(core == side)
                def _(side=side, it=it):
                    acc = lax.fori_loop(0, n_ev, later(side), (zero, zero))
                    settle(gath.at[it - 1, pl.ds(0, half)], f_recv.at[0])
                    acc = lax.fori_loop(0, n_ev, later(1 - side), acc)
                    sums[...] = acc[0] + acc[1]
        row = to_row(jnp.sum(sums[...], axis=1, keepdims=True))
        row = jnp.where(lanes[0:1] == freqs, count, row)
        if it == 0:
            pl.semaphore_wait(barrier, len(greeted))
        if it == 0:
            total = all_sum(0, ((stage_a, arecv_a.at[0], None), (stage_b, arecv_b.at[0], None)), row)
        else:
            total = all_sum_direct(row)
        number = jnp.sum(jnp.where(lanes[0:1] == freqs, total, 0.0), axis=1, keepdims=True)
        mean = to_column(total) / jnp.maximum(jnp.broadcast_to(number, (freqs, 1)), 1.0)
        limit = jnp.broadcast_to(1.345 * (1.2533 * mean + 1e-05), shape)

        for e in range(n_ev):
            sn[e] = zero
            sd[e] = zero

        def weigh(side, into, i):
            row = row_of(i)
            for j in range(0, X, 2):
                totals = [zero] * 4
                where = [side * half + across_x[j + u] + row for u in range(2)]
                for e in range(n_ev):
                    num = den = None
                    for u, t in enumerate(where):
                        r = rbuf[e, :, pl.ds(pl.multiple_of(t * LANES, LANES), LANES)]
                        w = limit * mask[e, t].astype(f32) / jnp.maximum(jnp.abs(r), limit)
                        p = w * r
                        totals[2 * u] += p
                        totals[2 * u + 1] += w
                        num = p if num is None else num + p
                        den = w if den is None else den + w
                    sn[e] += num
                    sd[e] += den
                for u in range(2):
                    into[X * i + j + u, 0] = totals[2 * u]
                    into[X * i + j + u, 1] = totals[2 * u + 1]

        def give(i, carry):
            weigh(1 - core, away.at[it], i)
            block = pl.ds(X * i, X)
            remote(away.at[it, block], recv_s.at[it, block], s_send.at[0], s_recv.at[i], sibling).start()
            return carry

        def take(i, carry):
            weigh(core, own.at[it], i)
            settle(recv_s.at[it, pl.ds(X * i, X)], s_recv.at[i])
            for j in (1, 0, 2, 3):
                p = X * i + j
                own[it, p] += recv_s[it, p]
                if j < X - 1:
                    peer = (across_x[j] + y_lo) * CORE + core
                    remote(own.at[it, p], recv_x.at[it, i, j], x_send.at[0], x_recv.at[i], (peer, ch)).start()
            return carry

        lax.fori_loop(0, Y_LO, give, 0)
        lax.fori_loop(0, Y_LO, take, 0)
        sent.append((recv_s.at[it], s_send.at[0]))
        sent.append((recv_x.at[it], x_send.at[0]))

        packed = zero
        for e in range(n_ev):
            packed = jnp.where(lanes == e, jnp.sum(sn[e], axis=1, keepdims=True), packed)
            packed = jnp.where(lanes == n_ev + e, jnp.sum(sd[e], axis=1, keepdims=True), packed)
        packed = packed[0:8] + pltpu.roll(packed[8:16], 2 * n_ev, axis=1)
        bsend[it, 0] = packed
        for k, peer in enumerate(along_z):
            remote(bsend.at[it, 0], brecv.at[it, k], b_send.at[0], b_recv.at[0], peer).start()
        sent.append((brecv.at[it], b_send.at[0]))

        for i in range(Y_LO):
            settle(recv_x.at[it, i], x_recv.at[i])
            both = tree([own[it, X * i + X - 1]] + [recv_x[it, i, j] for j in range(X - 1)])
            if i < Y_LO - 1:
                ysend[it, i] = both
                slot = lax.rem(row_of(i) + Y_LO - y_lo, Y_LO) - 1
                peer = (x * Y_LO + row_of(i)) * CORE + core
                remote(ysend.at[it, i], recv_y.at[it, slot], y_send.at[0], y_recv.at[0], (peer, ch)).start()
        sent.append((recv_y.at[it], y_send.at[0]))
        settle(brecv.at[it], b_recv.at[0])
        bsend[it, 1] = tree([bsend[it, 0]] + [brecv[it, k] for k in range(len(along_z))])
        remote(bsend.at[it, 1], brecv2.at[it], b_send.at[1], b_recv.at[1], across_y).start()
        sent.append((brecv2.at[it], b_send.at[1]))
        settle(recv_y.at[it], y_recv.at[0])
        both = tree([both] + [recv_y[it, i] for i in range(Y_LO - 1)])
        tile = core * half + chip
        gath[it, tile] = 0.5 * both[0] / (both[1] + 1.0)
        if it == ITERS - 1:
            final = site[:, pl.ds(pl.multiple_of(tile * LANES, LANES), LANES)]
            for i in range(ITERS):
                final = final + gath[i, tile]
            last_row = to_row(jnp.sum(final, axis=1, keepdims=True))

        def gather():
            for p in range(others):
                batch = 0 if p < NEAR else 1
                remote(
                    gath.at[it, tile], gath.at[it, tile], g_send.at[0], g_recv.at[batch],
                    (chip_at(p) * CORE + core, ch),
                ).start()
            remote(gath.at[it, tile], gath.at[it, tile], f_send.at[0], f_recv.at[0], sibling).start()
            sent.append((gath.at[it, pl.ds(0, others)], g_send.at[0]))
            sent.append((gath.at[it, pl.ds(0, half)], f_send.at[0]))

        def source_rest():
            settle(brecv2.at[it], b_recv.at[1])
            both = bsend[it, 1] + brecv2[it]
            use = lax.rem(lanes[0:8], 2 * n_ev) < n_ev
            below = jnp.where(use, pltpu.roll(both, LANES - n_ev, axis=1), 0.0)
            step = 0.5 * both / (below + 1.0)
            for e in range(n_ev):
                dsb[e, 0:8] = jnp.broadcast_to(step[:, e:e + 1], (8, LANES))
                dsb[e, 8:16] = jnp.broadcast_to(step[:, 2 * n_ev + e:2 * n_ev + e + 1], (8, LANES))
                srcb[e] += dsb[e]

        def forward():
            for batch, first, last in ((1, NEAR, others), (0, 0, NEAR)):
                settle(gath.at[it, pl.ds(0, last - first)], g_recv.at[batch])
                for p in range(first, last):
                    come = core * half + chip_from(p)
                    remote(gath.at[it, come], gath.at[it, come], f_send.at[0], f_recv.at[0], sibling).start()

        if it < ITERS - 1:
            gather()
            source_rest()
            forward()
        else:
            def finish():
                forward()
                source_rest()
                for e in range(n_ev):
                    out = to_row(srcb[e][:, 0:1])
                    source_o[e:e + 1, :] = out[:, 0:freqs]
                settle(gath.at[it, pl.ds(0, half)], f_recv.at[0])
                for t in range(tiles):
                    at = slice(t * LANES, (t + 1) * LANES)
                    site_o[:, at] = tree([site[:, at]] + [gath[i, t] for i in range(ITERS)])
            stages = (stage_a, arecv_a.at[1], gather), (stage_b, arecv_b.at[1], finish)
            total = all_sum(2, stages, last_row) * (1.0 / (n_ch * Y_HI * Z))

    shift = jnp.broadcast_to(to_column(total), shape)
    for t in range(tiles):
        at = slice(t * LANES, (t + 1) * LANES)
        site_o[:, at] = site_o[:, at] - shift
    source_o[...] = source_o[...] + jnp.broadcast_to(total[:, 0:freqs], (n_ev, freqs))
    drain()


def store(source, site, source_o, site_o, sem):
    copies = [
        pltpu.make_async_copy(src, dst, sem.at[i]) for i, (src, dst) in enumerate(((source, source_o), (site, site_o)))
    ]
    for copy in copies:
        copy.start()
    for copy in copies:
        copy.wait()


def on_device(spectra, tile_mask, source_init, site_init, event_pos, channel_pos, atten):
    n_ev, freqs, n_ch = spectra.shape
    tiles = n_ch // LANES
    half = tiles // 2
    assert half == CHIPS and freqs == n_ev == 16
    v, dma = pltpu.VMEM, pltpu.SemaphoreType.DMA
    na, nb = len(STAGE_A), len(STAGE_B)
    block = (freqs, LANES)
    scratch = [
        v((n_ev, freqs, n_ch), f32), v((freqs, n_ch), f32), v((2, n_ch), f32), v((n_ev, freqs), f32),
        v((1, freqs), f32), v((n_ev, tiles), jnp.int32),
        pltpu.SMEM((n_ev, tiles), jnp.int32), pltpu.SMEM((3, n_ev), f32),
        v((2, tiles, LANES), f32), v((n_ev,) + block, f32), v((n_ev,) + block, f32),
        v((n_ev,) + block, f32), v((n_ev,) + block, f32), v(block, f32),
        v((ITERS, half, 2) + block, f32), v((ITERS, half, 2) + block, f32), v((ITERS, half, 2) + block, f32),
        v((ITERS, Y_LO, X - 1, 2) + block, f32), v((ITERS, Y_LO - 1, 2) + block, f32), v((ITERS, Y_LO - 1, 2) + block, f32),
        v((ITERS, tiles) + block, f32),
        v((ITERS, 2, 8, LANES), f32), v((ITERS, Z - 1, 8, LANES), f32), v((ITERS, 8, LANES), f32),
        v((ITERS + 1, 2, 1, LANES), f32), v((1, 1, LANES), f32),
        v((2, na, 1, LANES), f32), v((2, nb, 1, LANES), f32), v((len(EVERYONE), 1, LANES), f32),
        dma((4,)), dma((7,)), dma((1,)), dma((Y_LO,)), dma((1,)), dma((Y_LO,)), dma((1,)), dma((1,)),
        dma((1,)), dma((2,)), dma((1,)), dma((1,)), dma((2,)), dma((2,)), dma((ITERS + 1, 2)), dma((ITERS + 1, 2)), dma((1,)), dma((1,)),
    ]
    hbm = pl.BlockSpec(memory_space=pltpu.HBM)
    vmem = pl.BlockSpec(memory_space=pltpu.VMEM)
    shapes = (jax.ShapeDtypeStruct((n_ev, freqs), f32), jax.ShapeDtypeStruct((freqs, n_ch), f32))
    inputs = (spectra, tile_mask, source_init, site_init, event_pos, channel_pos, atten.reshape(1, freqs))
    results = pl.pallas_call(
        kernel,
        out_shape=tuple(pltpu.VMEM(v.shape, f32) for v in shapes),
        in_specs=[hbm] * len(inputs),
        out_specs=(vmem, vmem),
        scratch_shapes=scratch,
        name="estimate",
        compiler_params=pltpu.CompilerParams(
            collective_id=0, has_side_effects=True, vmem_limit_bytes=40 << 20
        ),
    )(*[pltpu.with_memory_space_constraint(v, pltpu.HBM) for v in inputs])
    return pl.pallas_call(
        store,
        out_shape=shapes,
        in_specs=[vmem, vmem],
        out_specs=(hbm, hbm),
        scratch_shapes=[dma((2,))],
        name="store",
    )(*[pltpu.with_memory_space_constraint(v, pltpu.VMEM) for v in results])


def solution(mesh):
    in_specs = (
        P("ev", None, "ch"),
        P("ev", "ch"),
        P("ev", None),
        P(None, "ch"),
        P(None, "ev"),
        P(None, "ch"),
        P(),
    )
    out_specs = (P("ev", None), P(None, "ch"))
    return jax.shard_map(
        on_device, mesh=mesh, in_specs=in_specs, out_specs=out_specs, check_vma=False
    )
```

```python
import functools
import jax
import jax.numpy as jnp
from jax import lax
from jax.experimental import pallas as pl
from jax.experimental.pallas import tpu as pltpu
from jax.sharding import PartitionSpec as P

ITERS = 2
LANES = 128
X, Y_LO, CORE, Y_HI, Z = 4, 4, 2, 2, 8
Y = Y_HI * Y_LO
CHIPS = X * Y_LO
f32 = jnp.float32


def ring(step, size):
    return min(step, size - step)


STAGE_A = sorted(
    ((dz, dc) for dz in range(Z) for dc in range(CORE) if dz or dc),
    key=lambda s: -ring(s[0], Z),
)
STAGE_B = sorted(
    ((dy, dx) for dy in range(Y) for dx in range(X) if dy or dx),
    key=lambda s: -ring(s[0], Y) - ring(s[1], X),
)
EVERYONE = sorted(
    ((dx, dy, dz) for dx in range(X) for dy in range(Y) for dz in range(Z) if dx or dy or dz),
    key=lambda s: -ring(s[0], X) - ring(s[1], Y) - ring(s[2], Z),
)
NEAR = 8


def kernel(
    spectra, mask_h, source_h, site_h, event_h, channel_h, atten_h,
    source_o, site_o,
    rbuf, site, chan, srcv, attv, maskv, mask, evp, chx, srcb, dsb, sn, sd, sums,
    away, recv_s, own, recv_x, ysend, recv_y, gath, bsend, brecv, brecv2, arow, arecv_p, arecv_a, arecv_b, arecv_all,
    spec_sem, in_sem, s_send, s_recv, x_send, x_recv, y_send, y_recv, g_send, g_recv, f_send, f_recv,
    b_send, b_recv, a_send, a_recv, all_send, all_recv,
):
    n_ev, freqs, n_ch = rbuf.shape
    tiles = n_ch // LANES
    half = tiles // 2
    part = n_ev // 4
    others = half - 1
    ev, ch = lax.axis_index("ev"), lax.axis_index("ch")
    core, chip = lax.rem(ev, CORE), ev // CORE
    x, y_lo = chip // Y_LO, lax.rem(chip, Y_LO)
    y_hi, z = ch // Z, lax.rem(ch, Z)
    y = y_hi * Y_LO + y_lo

    def place(px, py, pz, pc):
        return ((px * Y_LO + lax.rem(py, Y_LO)) * CORE + pc, (py // Y_LO) * Z + pz)

    stage_a = [place(x, y, lax.rem(z + dz, Z), lax.rem(core + dc, CORE)) for dz, dc in STAGE_A]
    stage_b = [place(lax.rem(x + dx, X), lax.rem(y + dy, Y), z, core) for dy, dx in STAGE_B]
    sibling = (chip * CORE + 1 - core, ch)
    along_z = [(ev, y_hi * Z + lax.rem(z + dz, Z)) for dz in (4, 3, 5, 2, 6, 1, 7)]
    across_y = (ev, (1 - y_hi) * Z + z)

    upper, inner = y_lo // 2, lax.rem((y_lo + 1) // 2, 2)

    def row_of(i):
        there = (1 - upper) * (Y_LO - 1 - i) + upper * i
        return there + i // 2 * inner * (1 - 2 * lax.rem(there, 2))

    across_x = [lax.rem(x + j + 1, X) * Y_LO for j in range(X)]

    def chip_at(p):
        return across_x[p % X] + row_of(p // X)

    def chip_from(p):
        if p < NEAR:
            return p // 2 * Y_LO + 2 * (1 - upper) + p % 2
        if p < NEAR + X:
            return (p - NEAR) * Y_LO + y_lo + 1 - 2 * lax.rem(y_lo, 2)
        return across_x[p - NEAR - X] + y_lo

    barrier = pltpu.get_barrier_semaphore()
    greeted = stage_b + stage_a
    for peer in greeted:
        pl.semaphore_signal(barrier, inc=1, device_id=peer, device_id_type=pl.DeviceIdType.MESH)

    def remote(src, dst, send, recv, peer):
        return pltpu.make_async_remote_copy(
            src_ref=src, dst_ref=dst, send_sem=send, recv_sem=recv,
            device_id=peer, device_id_type=pl.DeviceIdType.MESH,
        )

    def settle(ref, sem):
        pltpu.make_async_copy(ref, ref, sem).wait()

    def spec_copy(q):
        return pltpu.make_async_copy(spectra.at[pl.ds(q * part, part)], rbuf.at[pl.ds(q * part, part)], spec_sem.at[q])

    small = [
        pltpu.make_async_copy(src, dst, in_sem.at[i])
        for i, (src, dst) in enumerate(
            [(mask_h, mask), (event_h, evp), (channel_h, chan), (atten_h, attv),
             (source_h, srcv), (mask_h, maskv), (site_h, site)]
        )
    ]
    for copy in small:
        copy.start()
    for q in range(n_ev // part):
        spec_copy(q).start()

    shape = (freqs, LANES)
    rows = lax.broadcasted_iota(jnp.int32, shape, 0)
    lanes = lax.broadcasted_iota(jnp.int32, shape, 1)
    diag = rows == lanes

    def to_column(row):
        spread = jnp.where(diag, jnp.broadcast_to(row, shape), 0.0)
        return jnp.sum(spread, axis=1, keepdims=True)

    def to_row(column):
        spread = jnp.where(diag, jnp.broadcast_to(column, shape), 0.0)
        return jnp.sum(spread, axis=0, keepdims=True)

    def tree(parts):
        while len(parts) > 1:
            parts = [a + b for a, b in zip(parts[::2], parts[1::2])] + parts[len(parts) // 2 * 2:]
        return parts[0]

    sent = []

    def drain():
        for ref, sem in sent:
            settle(ref, sem)
        sent.clear()

    def all_sum(turn, stages, row):
        for stage, (peers, landed, after) in enumerate(stages):
            arow[turn, stage] = row
            for k, peer in enumerate(peers):
                remote(arow.at[turn, stage], landed.at[k], a_send.at[turn, stage], a_recv.at[turn, stage], peer).start()
            sent.append((landed, a_send.at[turn, stage]))
            if after is not None:
                after()
            settle(landed, a_recv.at[turn, stage])
            row = tree([row] + [landed[k] for k in range(len(peers))])
        return row

    xs = [lax.rem(x + dx, X) for dx in range(X)]
    ys = [lax.rem(y + dy, Y) for dy in range(Y)]
    zs = [lax.rem(z + dz, Z) for dz in range(Z)]
    ev_at = [[(px * Y_LO + lax.rem(py, Y_LO)) * CORE + core for py in ys] for px in xs]
    ch_at = [[(py // Y_LO) * Z + pz for pz in zs] for py in ys]

    def all_sum_direct(row):
        row = all_sum(1, [([sibling], arecv_p, drain)], row)
        landed = arecv_all
        arow[1, 1] = row
        for k, (dx, dy, dz) in enumerate(EVERYONE):
            remote(arow.at[1, 1], arecv_all.at[k], all_send.at[0], all_recv.at[0], (ev_at[dx][dy], ch_at[dy][dz])).start()
        sent.append((landed, all_send.at[0]))
        settle(landed, all_recv.at[0])
        return tree([row] + [arecv_all[k] for k in range(len(EVERYONE))])

    for copy in small[:-1]:
        copy.wait()

    small_shape = (n_ev, freqs)
    small_diag = lax.broadcasted_iota(jnp.int32, small_shape, 0) == lax.broadcasted_iota(jnp.int32, small_shape, 1)

    def widen(row):
        spread = jnp.where(small_diag, jnp.broadcast_to(row, small_shape), 0.0)
        return jnp.broadcast_to(jnp.sum(spread, axis=1, keepdims=True), shape)

    for t in range(tiles):
        chx[0, t:t + 1, :] = chan[0:1, t * LANES:(t + 1) * LANES]
        chx[1, t:t + 1, :] = chan[1:2, t * LANES:(t + 1) * LANES]
    for e in range(n_ev):
        srcb[e] = widen(srcv[e:e + 1, :])
    attb = widen(attv[0:1, :])
    count = float(LANES) * jnp.sum(maskv[...].astype(f32), keepdims=True)

    small[-1].wait()
    zero = jnp.zeros(shape, f32)
    for it in range(ITERS):
        def first(e, carry):
            accs = list(carry)

            @pl.when(lax.rem(e, part) == 0)
            def _():
                spec_copy(e // part).wait()
            east = evp[0, e] - chx[0]
            north = evp[1, e] - chx[1]
            travel = jnp.sqrt(east * east + north * north + evp[2, e] * evp[2, e]) * (1.0 / 3.0)
            for t in range(tiles):
                at = slice(t * LANES, (t + 1) * LANES)
                r = rbuf[e, :, at] - srcb[e] - site[:, at] + attb * jnp.broadcast_to(travel[t:t + 1, :], shape)
                rbuf[e, :, at] = r
                accs[t % 2] = accs[t % 2] + jnp.abs(r) * mask[e, t].astype(f32)
            return tuple(accs)

        def later(side, it=it):
            def update(e, carry):
                accs = list(carry)
                for t in range(side * half, (side + 1) * half):
                    at = slice(t * LANES, (t + 1) * LANES)
                    r = rbuf[e, :, at] - dsb[e] - gath[it - 1, t]
                    rbuf[e, :, at] = r
                    accs[t % 2] = accs[t % 2] + jnp.abs(r) * mask[e, t].astype(f32)
                return tuple(accs)
            return update

        if it == 0:
            first_sum, second_sum = lax.fori_loop(0, n_ev, first, (zero, zero))
            sums[...] = first_sum + second_sum
        else:
            for side in range(CORE):
                @pl.when(core == side)
                def _(side=side, it=it):
                    acc = lax.fori_loop(0, n_ev, later(side), (zero, zero))
                    settle(gath.at[it - 1, pl.ds(0, half)], f_recv.at[0])
                    acc = lax.fori_loop(0, n_ev, later(1 - side), acc)
                    sums[...] = acc[0] + acc[1]
        row = to_row(jnp.sum(sums[...], axis=1, keepdims=True))
        row = jnp.where(lanes[0:1] == freqs, count, row)
        if it == 0:
            pl.semaphore_wait(barrier, len(greeted))
        if it == 0:
            total = all_sum(0, ((stage_a, arecv_a.at[0], None), (stage_b, arecv_b.at[0], None)), row)
        else:
            total = all_sum_direct(row)
        number = jnp.sum(jnp.where(lanes[0:1] == freqs, total, 0.0), axis=1, keepdims=True)
        mean = to_column(total) / jnp.maximum(jnp.broadcast_to(number, (freqs, 1)), 1.0)
        limit = jnp.broadcast_to(1.345 * (1.2533 * mean + 1e-05), shape)

        for e in range(n_ev):
            sn[e] = zero
            sd[e] = zero

        def weigh(side, into, i):
            row = row_of(i)
            for j in range(0, X, 2):
                totals = [zero] * 4
                where = [side * half + across_x[j + u] + row for u in range(2)]
                for e in range(n_ev):
                    num = den = None
                    for u, t in enumerate(where):
                        r = rbuf[e, :, pl.ds(pl.multiple_of(t * LANES, LANES), LANES)]
                        w = limit * mask[e, t].astype(f32) / jnp.maximum(jnp.abs(r), limit)
                        p = w * r
                        totals[2 * u] += p
                        totals[2 * u + 1] += w
                        num = p if num is None else num + p
                        den = w if den is None else den + w
                    sn[e] += num
                    sd[e] += den
                for u in range(2):
                    into[X * i + j + u, 0] = totals[2 * u]
                    into[X * i + j + u, 1] = totals[2 * u + 1]

        def give(i, carry):
            weigh(1 - core, away.at[it], i)
            block = pl.ds(X * i, X)
            remote(away.at[it, block], recv_s.at[it, block], s_send.at[0], s_recv.at[i], sibling).start()
            return carry

        def take(i, carry):
            weigh(core, own.at[it], i)
            settle(recv_s.at[it, pl.ds(X * i, X)], s_recv.at[i])
            for j in (1, 0, 2, 3):
                p = X * i + j
                own[it, p] += recv_s[it, p]
                if j < X - 1:
                    peer = (across_x[j] + y_lo) * CORE + core
                    remote(own.at[it, p], recv_x.at[it, i, j], x_send.at[0], x_recv.at[i], (peer, ch)).start()
            return carry

        lax.fori_loop(0, Y_LO, give, 0)
        lax.fori_loop(0, Y_LO, take, 0)
        sent.append((recv_s.at[it], s_send.at[0]))
        sent.append((recv_x.at[it], x_send.at[0]))

        packed = zero
        for e in range(n_ev):
            packed = jnp.where(lanes == e, jnp.sum(sn[e], axis=1, keepdims=True), packed)
            packed = jnp.where(lanes == n_ev + e, jnp.sum(sd[e], axis=1, keepdims=True), packed)
        packed = packed[0:8] + pltpu.roll(packed[8:16], 2 * n_ev, axis=1)
        bsend[it, 0] = packed
        for k, peer in enumerate(along_z):
            remote(bsend.at[it, 0], brecv.at[it, k], b_send.at[0], b_recv.at[0], peer).start()
        sent.append((brecv.at[it], b_send.at[0]))

        for i in range(Y_LO):
            settle(recv_x.at[it, i], x_recv.at[i])
            both = tree([own[it, X * i + X - 1]] + [recv_x[it, i, j] for j in range(X - 1)])
            if i < Y_LO - 1:
                ysend[it, i] = both
                slot = lax.rem(row_of(i) + Y_LO - y_lo, Y_LO) - 1
                peer = (x * Y_LO + row_of(i)) * CORE + core
                remote(ysend.at[it, i], recv_y.at[it, slot], y_send.at[0], y_recv.at[0], (peer, ch)).start()
        sent.append((recv_y.at[it], y_send.at[0]))
        settle(brecv.at[it], b_recv.at[0])
        bsend[it, 1] = tree([bsend[it, 0]] + [brecv[it, k] for k in range(len(along_z))])
        remote(bsend.at[it, 1], brecv2.at[it], b_send.at[1], b_recv.at[1], across_y).start()
        sent.append((brecv2.at[it], b_send.at[1]))
        settle(recv_y.at[it], y_recv.at[0])
        both = tree([both] + [recv_y[it, i] for i in range(Y_LO - 1)])
        tile = core * half + chip
        gath[it, tile] = 0.5 * both[0] / (both[1] + 1.0)
        if it == ITERS - 1:
            final = site[:, pl.ds(pl.multiple_of(tile * LANES, LANES), LANES)]
            for i in range(ITERS):
                final = final + gath[i, tile]
            last_row = to_row(jnp.sum(final, axis=1, keepdims=True))

        def gather():
            for p in range(others):
                batch = 0 if p < NEAR else 1
                remote(
                    gath.at[it, tile], gath.at[it, tile], g_send.at[0], g_recv.at[batch],
                    (chip_at(p) * CORE + core, ch),
                ).start()
            remote(gath.at[it, tile], gath.at[it, tile], f_send.at[0], f_recv.at[0], sibling).start()
            sent.append((gath.at[it, pl.ds(0, others)], g_send.at[0]))
            sent.append((gath.at[it, pl.ds(0, half)], f_send.at[0]))

        def source_rest():
            settle(brecv2.at[it], b_recv.at[1])
            both = bsend[it, 1] + brecv2[it]
            use = lax.rem(lanes[0:8], 2 * n_ev) < n_ev
            below = jnp.where(use, pltpu.roll(both, LANES - n_ev, axis=1), 0.0)
            step = 0.5 * both / (below + 1.0)
            for e in range(n_ev):
                dsb[e, 0:8] = jnp.broadcast_to(step[:, e:e + 1], (8, LANES))
                dsb[e, 8:16] = jnp.broadcast_to(step[:, 2 * n_ev + e:2 * n_ev + e + 1], (8, LANES))
                srcb[e] += dsb[e]

        def forward():
            for batch, first, last in ((1, NEAR, others), (0, 0, NEAR)):
                settle(gath.at[it, pl.ds(0, last - first)], g_recv.at[batch])
                for p in range(first, last):
                    come = core * half + chip_from(p)
                    remote(gath.at[it, come], gath.at[it, come], f_send.at[0], f_recv.at[0], sibling).start()

        if it < ITERS - 1:
            gather()
            source_rest()
            forward()
        else:
            def finish():
                forward()
                source_rest()
                for e in range(n_ev):
                    out = to_row(srcb[e][:, 0:1])
                    source_o[e:e + 1, :] = out[:, 0:freqs]
                settle(gath.at[it, pl.ds(0, half)], f_recv.at[0])
                for t in range(tiles):
                    at = slice(t * LANES, (t + 1) * LANES)
                    site_o[:, at] = tree([site[:, at]] + [gath[i, t] for i in range(ITERS)])
            stages = (stage_a, arecv_a.at[1], gather), (stage_b, arecv_b.at[1], finish)
            total = all_sum(2, stages, last_row) * (1.0 / (n_ch * Y_HI * Z))

    shift = jnp.broadcast_to(to_column(total), shape)
    for t in range(tiles):
        at = slice(t * LANES, (t + 1) * LANES)
        site_o[:, at] = site_o[:, at] - shift
    source_o[...] = source_o[...] + jnp.broadcast_to(total[:, 0:freqs], (n_ev, freqs))
    drain()


def store(source, site, source_o, site_o, sem):
    copies = [
        pltpu.make_async_copy(src, dst, sem.at[i]) for i, (src, dst) in enumerate(((source, source_o), (site, site_o)))
    ]
    for copy in copies:
        copy.start()
    for copy in copies:
        copy.wait()


def on_device(spectra, tile_mask, source_init, site_init, event_pos, channel_pos, atten):
    n_ev, freqs, n_ch = spectra.shape
    tiles = n_ch // LANES
    half = tiles // 2
    assert half == CHIPS and freqs == n_ev == 16
    v, dma = pltpu.VMEM, pltpu.SemaphoreType.DMA
    na, nb = len(STAGE_A), len(STAGE_B)
    block = (freqs, LANES)
    scratch = [
        v((n_ev, freqs, n_ch), f32), v((freqs, n_ch), f32), v((2, n_ch), f32), v((n_ev, freqs), f32),
        v((1, freqs), f32), v((n_ev, tiles), jnp.int32),
        pltpu.SMEM((n_ev, tiles), jnp.int32), pltpu.SMEM((3, n_ev), f32),
        v((2, tiles, LANES), f32), v((n_ev,) + block, f32), v((n_ev,) + block, f32),
        v((n_ev,) + block, f32), v((n_ev,) + block, f32), v(block, f32),
        v((ITERS, half, 2) + block, f32), v((ITERS, half, 2) + block, f32), v((ITERS, half, 2) + block, f32),
        v((ITERS, Y_LO, X - 1, 2) + block, f32), v((ITERS, Y_LO - 1, 2) + block, f32), v((ITERS, Y_LO - 1, 2) + block, f32),
        v((ITERS, tiles) + block, f32),
        v((ITERS, 2, 8, LANES), f32), v((ITERS, Z - 1, 8, LANES), f32), v((ITERS, 8, LANES), f32),
        v((ITERS + 1, 2, 1, LANES), f32), v((1, 1, LANES), f32),
        v((2, na, 1, LANES), f32), v((2, nb, 1, LANES), f32), v((len(EVERYONE), 1, LANES), f32),
        dma((4,)), dma((7,)), dma((1,)), dma((Y_LO,)), dma((1,)), dma((Y_LO,)), dma((1,)), dma((1,)),
        dma((1,)), dma((2,)), dma((1,)), dma((1,)), dma((2,)), dma((2,)), dma((ITERS + 1, 2)), dma((ITERS + 1, 2)), dma((1,)), dma((1,)),
    ]
    hbm = pl.BlockSpec(memory_space=pltpu.HBM)
    vmem = pl.BlockSpec(memory_space=pltpu.VMEM)
    shapes = (jax.ShapeDtypeStruct((n_ev, freqs), f32), jax.ShapeDtypeStruct((freqs, n_ch), f32))
    inputs = (spectra, tile_mask, source_init, site_init, event_pos, channel_pos, atten.reshape(1, freqs))
    results = pl.pallas_call(
        kernel,
        out_shape=tuple(pltpu.VMEM(v.shape, f32) for v in shapes),
        in_specs=[hbm] * len(inputs),
        out_specs=(vmem, vmem),
        scratch_shapes=scratch,
        name="estimate",
        compiler_params=pltpu.CompilerParams(
            collective_id=0, has_side_effects=True, vmem_limit_bytes=40 << 20
        ),
    )(*[pltpu.with_memory_space_constraint(v, pltpu.HBM) for v in inputs])
    return pl.pallas_call(
        store,
        out_shape=shapes,
        in_specs=[vmem, vmem],
        out_specs=(hbm, hbm),
        scratch_shapes=[dma((2,))],
        name="store",
    )(*[pltpu.with_memory_space_constraint(v, pltpu.VMEM) for v in results])


def solution(mesh):
    in_specs = (
        P("ev", None, "ch"),
        P("ev", "ch"),
        P("ev", None),
        P(None, "ch"),
        P(None, "ev"),
        P(None, "ch"),
        P(),
    )
    out_specs = (P("ev", None), P(None, "ch"))
    return jax.shard_map(
        on_device, mesh=mesh, in_specs=in_specs, out_specs=out_specs, check_vma=False
    )
```

```python
import functools
import jax
import jax.numpy as jnp
from jax import lax
from jax.experimental import pallas as pl
from jax.experimental.pallas import tpu as pltpu
from jax.sharding import PartitionSpec as P

ITERS = 2
LANES = 128
X, Y_LO, CORE, Y_HI, Z = 4, 4, 2, 2, 8
Y = Y_HI * Y_LO
CHIPS = X * Y_LO
f32 = jnp.float32


def ring(step, size):
    return min(step, size - step)


STAGE_A = sorted(
    ((dz, dc) for dz in range(Z) for dc in range(CORE) if dz or dc),
    key=lambda s: -ring(s[0], Z),
)
STAGE_B = sorted(
    ((dy, dx) for dy in range(Y) for dx in range(X) if dy or dx),
    key=lambda s: -ring(s[0], Y) - ring(s[1], X),
)
EVERYONE = sorted(
    ((dx, dy, dz) for dx in range(X) for dy in range(Y) for dz in range(Z) if dx or dy or dz),
    key=lambda s: -ring(s[0], X) - ring(s[1], Y) - ring(s[2], Z),
)
NEAR = 8


def kernel(
    spectra, mask_h, source_h, site_h, event_h, channel_h, atten_h,
    source_o, site_o,
    rbuf, site, chan, srcv, attv, maskv, mask, evp, chx, srcb, dsb, sn, sd, sums, kept,
    away, recv_s, own, recv_x, ysend, recv_y, gath, bsend, brecv, brecv2, arow, arecv_p, arecv_a, arecv_b, arecv_all,
    spec_sem, in_sem, s_send, s_recv, x_send, x_recv, y_send, y_recv, g_send, g_recv, f_send, f_recv,
    b_send, b_recv, a_send, a_recv, all_send, all_recv,
):
    n_ev, freqs, n_ch = rbuf.shape
    tiles = n_ch // LANES
    half = tiles // 2
    part = n_ev // 4
    others = half - 1
    ev, ch = lax.axis_index("ev"), lax.axis_index("ch")
    core, chip = lax.rem(ev, CORE), ev // CORE
    x, y_lo = chip // Y_LO, lax.rem(chip, Y_LO)
    y_hi, z = ch // Z, lax.rem(ch, Z)
    y = y_hi * Y_LO + y_lo

    def place(px, py, pz, pc):
        return ((px * Y_LO + lax.rem(py, Y_LO)) * CORE + pc, (py // Y_LO) * Z + pz)

    stage_a = [place(x, y, lax.rem(z + dz, Z), lax.rem(core + dc, CORE)) for dz, dc in STAGE_A]
    stage_b = [place(lax.rem(x + dx, X), lax.rem(y + dy, Y), z, core) for dy, dx in STAGE_B]
    sibling = (chip * CORE + 1 - core, ch)
    along_z = [(ev, y_hi * Z + lax.rem(z + dz, Z)) for dz in (4, 3, 5, 2, 6, 1, 7)]
    across_y = (ev, (1 - y_hi) * Z + z)

    upper, inner = y_lo // 2, lax.rem((y_lo + 1) // 2, 2)

    def row_of(i):
        there = (1 - upper) * (Y_LO - 1 - i) + upper * i
        return there + i // 2 * inner * (1 - 2 * lax.rem(there, 2))

    across_x = [lax.rem(x + j + 1, X) * Y_LO for j in range(X)]

    def chip_at(p):
        return across_x[p % X] + row_of(p // X)

    def chip_from(p):
        if p < NEAR:
            return p // 2 * Y_LO + 2 * (1 - upper) + p % 2
        if p < NEAR + X:
            return (p - NEAR) * Y_LO + y_lo + 1 - 2 * lax.rem(y_lo, 2)
        return across_x[p - NEAR - X] + y_lo

    barrier = pltpu.get_barrier_semaphore()
    greeted = stage_b + stage_a
    for peer in greeted:
        pl.semaphore_signal(barrier, inc=1, device_id=peer, device_id_type=pl.DeviceIdType.MESH)

    def remote(src, dst, send, recv, peer):
        return pltpu.make_async_remote_copy(
            src_ref=src, dst_ref=dst, send_sem=send, recv_sem=recv,
            device_id=peer, device_id_type=pl.DeviceIdType.MESH,
        )

    def settle(ref, sem):
        pltpu.make_async_copy(ref, ref, sem).wait()

    def spec_copy(q):
        return pltpu.make_async_copy(spectra.at[pl.ds(q * part, part)], rbuf.at[pl.ds(q * part, part)], spec_sem.at[q])

    small = [
        pltpu.make_async_copy(src, dst, in_sem.at[i])
        for i, (src, dst) in enumerate(
            [(mask_h, mask), (event_h, evp), (channel_h, chan), (atten_h, attv),
             (source_h, srcv), (mask_h, maskv), (site_h, site)]
        )
    ]
    for copy in small:
        copy.start()
    for q in range(n_ev // part):
        spec_copy(q).start()

    shape = (freqs, LANES)
    rows = lax.broadcasted_iota(jnp.int32, shape, 0)
    lanes = lax.broadcasted_iota(jnp.int32, shape, 1)
    diag = rows == lanes

    def to_column(row):
        spread = jnp.where(diag, jnp.broadcast_to(row, shape), 0.0)
        return jnp.sum(spread, axis=1, keepdims=True)

    def to_row(column):
        spread = jnp.where(diag, jnp.broadcast_to(column, shape), 0.0)
        return jnp.sum(spread, axis=0, keepdims=True)

    def tree(parts):
        while len(parts) > 1:
            parts = [a + b for a, b in zip(parts[::2], parts[1::2])] + parts[len(parts) // 2 * 2:]
        return parts[0]

    sent = []

    def drain():
        for ref, sem in sent:
            settle(ref, sem)
        sent.clear()

    def all_sum(turn, stages, row):
        for stage, (peers, landed, after) in enumerate(stages):
            arow[turn, stage] = row
            for k, peer in enumerate(peers):
                remote(arow.at[turn, stage], landed.at[k], a_send.at[turn, stage], a_recv.at[turn, stage], peer).start()
            sent.append((landed, a_send.at[turn, stage]))
            if after is not None:
                after()
            settle(landed, a_recv.at[turn, stage])
            row = tree([row] + [landed[k] for k in range(len(peers))])
        return row

    xs = [lax.rem(x + dx, X) for dx in range(X)]
    ys = [lax.rem(y + dy, Y) for dy in range(Y)]
    zs = [lax.rem(z + dz, Z) for dz in range(Z)]
    ev_at = [[(px * Y_LO + lax.rem(py, Y_LO)) * CORE + core for py in ys] for px in xs]
    ch_at = [[(py // Y_LO) * Z + pz for pz in zs] for py in ys]

    def all_sum_direct(row):
        row = all_sum(1, [([sibling], arecv_p, drain)], row)
        landed = arecv_all
        arow[1, 1] = row
        for k, (dx, dy, dz) in enumerate(EVERYONE):
            remote(arow.at[1, 1], arecv_all.at[k], all_send.at[0], all_recv.at[0], (ev_at[dx][dy], ch_at[dy][dz])).start()
        sent.append((landed, all_send.at[0]))
        settle(landed, all_recv.at[0])
        return tree([row] + [arecv_all[k] for k in range(len(EVERYONE))])

    for copy in small[:-1]:
        copy.wait()

    small_shape = (n_ev, freqs)
    small_diag = lax.broadcasted_iota(jnp.int32, small_shape, 0) == lax.broadcasted_iota(jnp.int32, small_shape, 1)

    def widen(row):
        spread = jnp.where(small_diag, jnp.broadcast_to(row, small_shape), 0.0)
        return jnp.broadcast_to(jnp.sum(spread, axis=1, keepdims=True), shape)

    for t in range(tiles):
        chx[0, t:t + 1, :] = chan[0:1, t * LANES:(t + 1) * LANES]
        chx[1, t:t + 1, :] = chan[1:2, t * LANES:(t + 1) * LANES]
    for e in range(n_ev):
        srcb[e] = widen(srcv[e:e + 1, :])
    attb = widen(attv[0:1, :])
    count = float(LANES) * jnp.sum(maskv[...].astype(f32), keepdims=True)

    small[-1].wait()
    zero = jnp.zeros(shape, f32)

    def spread_mask():
        flags = maskv[...].astype(f32)
        for t in range(tiles):
            kept[t] = jnp.broadcast_to(flags[:, t:t + 1], (n_ev, LANES))

    for it in range(ITERS):
        def first(e, carry):
            accs = list(carry)

            @pl.when(lax.rem(e, part) == 0)
            def _():
                spec_copy(e // part).wait()
            east = evp[0, e] - chx[0]
            north = evp[1, e] - chx[1]
            travel = jnp.sqrt(east * east + north * north + evp[2, e] * evp[2, e]) * (1.0 / 3.0)
            for t in range(tiles):
                at = slice(t * LANES, (t + 1) * LANES)
                r = rbuf[e, :, at] - srcb[e] - site[:, at] + attb * jnp.broadcast_to(travel[t:t + 1, :], shape)
                rbuf[e, :, at] = r
                accs[t % 2] = accs[t % 2] + jnp.abs(r) * mask[e, t].astype(f32)
            return tuple(accs)

        def later(side, it=it):
            def update(e, carry):
                accs = list(carry)
                for t in range(side * half, (side + 1) * half):
                    at = slice(t * LANES, (t + 1) * LANES)
                    r = rbuf[e, :, at] - dsb[e] - gath[it - 1, t]
                    rbuf[e, :, at] = r
                    accs[t % 2] = accs[t % 2] + jnp.abs(r) * mask[e, t].astype(f32)
                return tuple(accs)
            return update

        if it == 0:
            first_sum, second_sum = lax.fori_loop(0, n_ev, first, (zero, zero))
            sums[...] = first_sum + second_sum
        else:
            for side in range(CORE):
                @pl.when(core == side)
                def _(side=side, it=it):
                    acc = lax.fori_loop(0, n_ev, later(side), (zero, zero))
                    settle(gath.at[it - 1, pl.ds(0, half)], f_recv.at[0])
                    acc = lax.fori_loop(0, n_ev, later(1 - side), acc)
                    sums[...] = acc[0] + acc[1]
        row = to_row(jnp.sum(sums[...], axis=1, keepdims=True))
        row = jnp.where(lanes[0:1] == freqs, count, row)
        if it == 0:
            pl.semaphore_wait(barrier, len(greeted))
        if it == 0:
            total = all_sum(0, ((stage_a, arecv_a.at[0], spread_mask), (stage_b, arecv_b.at[0], None)), row)
        else:
            total = all_sum_direct(row)
        number = jnp.sum(jnp.where(lanes[0:1] == freqs, total, 0.0), axis=1, keepdims=True)
        mean = to_column(total) / jnp.maximum(jnp.broadcast_to(number, (freqs, 1)), 1.0)
        limit = jnp.broadcast_to(1.345 * (1.2533 * mean + 1e-05), shape)

        for e in range(n_ev):
            sn[e] = zero
            sd[e] = zero

        def weigh(side, into, i):
            row = row_of(i)
            for j in range(0, X, 2):
                totals = [zero] * 4
                where = [side * half + across_x[j + u] + row for u in range(2)]
                for e in range(n_ev):
                    num = den = None
                    for u, t in enumerate(where):
                        r = rbuf[e, :, pl.ds(pl.multiple_of(t * LANES, LANES), LANES)]
                        w = limit * jnp.broadcast_to(kept[t, e:e + 1, :], shape) / jnp.maximum(jnp.abs(r), limit)
                        p = w * r
                        totals[2 * u] += p
                        totals[2 * u + 1] += w
                        num = p if num is None else num + p
                        den = w if den is None else den + w
                    sn[e] += num
                    sd[e] += den
                for u in range(2):
                    into[X * i + j + u, 0] = totals[2 * u]
                    into[X * i + j + u, 1] = totals[2 * u + 1]

        def give(i, carry):
            weigh(1 - core, away.at[it], i)
            block = pl.ds(X * i, X)
            remote(away.at[it, block], recv_s.at[it, block], s_send.at[0], s_recv.at[i], sibling).start()
            return carry

        def take(i, carry):
            weigh(core, own.at[it], i)
            settle(recv_s.at[it, pl.ds(X * i, X)], s_recv.at[i])
            for j in (1, 0, 2, 3):
                p = X * i + j
                own[it, p] += recv_s[it, p]
                if j < X - 1:
                    peer = (across_x[j] + y_lo) * CORE + core
                    remote(own.at[it, p], recv_x.at[it, i, j], x_send.at[0], x_recv.at[i], (peer, ch)).start()
            return carry

        lax.fori_loop(0, Y_LO, give, 0)
        lax.fori_loop(0, Y_LO, take, 0)
        sent.append((recv_s.at[it], s_send.at[0]))
        sent.append((recv_x.at[it], x_send.at[0]))

        packed = zero
        for e in range(n_ev):
            packed = jnp.where(lanes == e, jnp.sum(sn[e], axis=1, keepdims=True), packed)
            packed = jnp.where(lanes == n_ev + e, jnp.sum(sd[e], axis=1, keepdims=True), packed)
        packed = packed[0:8] + pltpu.roll(packed[8:16], 2 * n_ev, axis=1)
        bsend[it, 0] = packed
        for k, peer in enumerate(along_z):
            remote(bsend.at[it, 0], brecv.at[it, k], b_send.at[0], b_recv.at[0], peer).start()
        sent.append((brecv.at[it], b_send.at[0]))

        for i in range(Y_LO):
            settle(recv_x.at[it, i], x_recv.at[i])
            both = tree([own[it, X * i + X - 1]] + [recv_x[it, i, j] for j in range(X - 1)])
            if i < Y_LO - 1:
                ysend[it, i] = both
                slot = lax.rem(row_of(i) + Y_LO - y_lo, Y_LO) - 1
                peer = (x * Y_LO + row_of(i)) * CORE + core
                remote(ysend.at[it, i], recv_y.at[it, slot], y_send.at[0], y_recv.at[0], (peer, ch)).start()
        sent.append((recv_y.at[it], y_send.at[0]))
        settle(brecv.at[it], b_recv.at[0])
        bsend[it, 1] = tree([bsend[it, 0]] + [brecv[it, k] for k in range(len(along_z))])
        remote(bsend.at[it, 1], brecv2.at[it], b_send.at[1], b_recv.at[1], across_y).start()
        sent.append((brecv2.at[it], b_send.at[1]))
        settle(recv_y.at[it], y_recv.at[0])
        both = tree([both] + [recv_y[it, i] for i in range(Y_LO - 1)])
        tile = core * half + chip
        gath[it, tile] = 0.5 * both[0] / (both[1] + 1.0)
        if it == ITERS - 1:
            final = site[:, pl.ds(pl.multiple_of(tile * LANES, LANES), LANES)]
            for i in range(ITERS):
                final = final + gath[i, tile]
            last_row = to_row(jnp.sum(final, axis=1, keepdims=True))

        def gather():
            for p in range(others):
                batch = 0 if p < NEAR else 1
                remote(
                    gath.at[it, tile], gath.at[it, tile], g_send.at[0], g_recv.at[batch],
                    (chip_at(p) * CORE + core, ch),
                ).start()
            remote(gath.at[it, tile], gath.at[it, tile], f_send.at[0], f_recv.at[0], sibling).start()
            sent.append((gath.at[it, pl.ds(0, others)], g_send.at[0]))
            sent.append((gath.at[it, pl.ds(0, half)], f_send.at[0]))

        def source_rest():
            settle(brecv2.at[it], b_recv.at[1])
            both = bsend[it, 1] + brecv2[it]
            use = lax.rem(lanes[0:8], 2 * n_ev) < n_ev
            below = jnp.where(use, pltpu.roll(both, LANES - n_ev, axis=1), 0.0)
            step = 0.5 * both / (below + 1.0)
            for e in range(n_ev):
                dsb[e, 0:8] = jnp.broadcast_to(step[:, e:e + 1], (8, LANES))
                dsb[e, 8:16] = jnp.broadcast_to(step[:, 2 * n_ev + e:2 * n_ev + e + 1], (8, LANES))
                srcb[e] += dsb[e]

        def forward():
            for batch, first, last in ((1, NEAR, others), (0, 0, NEAR)):
                settle(gath.at[it, pl.ds(0, last - first)], g_recv.at[batch])
                for p in range(first, last):
                    come = core * half + chip_from(p)
                    remote(gath.at[it, come], gath.at[it, come], f_send.at[0], f_recv.at[0], sibling).start()

        if it < ITERS - 1:
            gather()
            source_rest()
            forward()
        else:
            def finish():
                forward()
                source_rest()
                for e in range(n_ev):
                    out = to_row(srcb[e][:, 0:1])
                    source_o[e:e + 1, :] = out[:, 0:freqs]
                settle(gath.at[it, pl.ds(0, half)], f_recv.at[0])
                for t in range(tiles):
                    at = slice(t * LANES, (t + 1) * LANES)
                    site_o[:, at] = tree([site[:, at]] + [gath[i, t] for i in range(ITERS)])
            stages = (stage_a, arecv_a.at[1], gather), (stage_b, arecv_b.at[1], finish)
            total = all_sum(2, stages, last_row) * (1.0 / (n_ch * Y_HI * Z))

    shift = jnp.broadcast_to(to_column(total), shape)
    for t in range(tiles):
        at = slice(t * LANES, (t + 1) * LANES)
        site_o[:, at] = site_o[:, at] - shift
    source_o[...] = source_o[...] + jnp.broadcast_to(total[:, 0:freqs], (n_ev, freqs))
    drain()


def store(source, site, source_o, site_o, sem):
    copies = [
        pltpu.make_async_copy(src, dst, sem.at[i]) for i, (src, dst) in enumerate(((source, source_o), (site, site_o)))
    ]
    for copy in copies:
        copy.start()
    for copy in copies:
        copy.wait()


def on_device(spectra, tile_mask, source_init, site_init, event_pos, channel_pos, atten):
    n_ev, freqs, n_ch = spectra.shape
    tiles = n_ch // LANES
    half = tiles // 2
    assert half == CHIPS and freqs == n_ev == 16
    v, dma = pltpu.VMEM, pltpu.SemaphoreType.DMA
    na, nb = len(STAGE_A), len(STAGE_B)
    block = (freqs, LANES)
    scratch = [
        v((n_ev, freqs, n_ch), f32), v((freqs, n_ch), f32), v((2, n_ch), f32), v((n_ev, freqs), f32),
        v((1, freqs), f32), v((n_ev, tiles), jnp.int32),
        pltpu.SMEM((n_ev, tiles), jnp.int32), pltpu.SMEM((3, n_ev), f32),
        v((2, tiles, LANES), f32), v((n_ev,) + block, f32), v((n_ev,) + block, f32),
        v((n_ev,) + block, f32), v((n_ev,) + block, f32), v(block, f32), v((tiles, n_ev, LANES), f32),
        v((ITERS, half, 2) + block, f32), v((ITERS, half, 2) + block, f32), v((ITERS, half, 2) + block, f32),
        v((ITERS, Y_LO, X - 1, 2) + block, f32), v((ITERS, Y_LO - 1, 2) + block, f32), v((ITERS, Y_LO - 1, 2) + block, f32),
        v((ITERS, tiles) + block, f32),
        v((ITERS, 2, 8, LANES), f32), v((ITERS, Z - 1, 8, LANES), f32), v((ITERS, 8, LANES), f32),
        v((ITERS + 1, 2, 1, LANES), f32), v((1, 1, LANES), f32),
        v((2, na, 1, LANES), f32), v((2, nb, 1, LANES), f32), v((len(EVERYONE), 1, LANES), f32),
        dma((4,)), dma((7,)), dma((1,)), dma((Y_LO,)), dma((1,)), dma((Y_LO,)), dma((1,)), dma((1,)),
        dma((1,)), dma((2,)), dma((1,)), dma((1,)), dma((2,)), dma((2,)), dma((ITERS + 1, 2)), dma((ITERS + 1, 2)), dma((1,)), dma((1,)),
    ]
    hbm = pl.BlockSpec(memory_space=pltpu.HBM)
    vmem = pl.BlockSpec(memory_space=pltpu.VMEM)
    shapes = (jax.ShapeDtypeStruct((n_ev, freqs), f32), jax.ShapeDtypeStruct((freqs, n_ch), f32))
    inputs = (spectra, tile_mask, source_init, site_init, event_pos, channel_pos, atten.reshape(1, freqs))
    results = pl.pallas_call(
        kernel,
        out_shape=tuple(pltpu.VMEM(v.shape, f32) for v in shapes),
        in_specs=[hbm] * len(inputs),
        out_specs=(vmem, vmem),
        scratch_shapes=scratch,
        name="estimate",
        compiler_params=pltpu.CompilerParams(
            collective_id=0, has_side_effects=True, vmem_limit_bytes=40 << 20
        ),
    )(*[pltpu.with_memory_space_constraint(v, pltpu.HBM) for v in inputs])
    return pl.pallas_call(
        store,
        out_shape=shapes,
        in_specs=[vmem, vmem],
        out_specs=(hbm, hbm),
        scratch_shapes=[dma((2,))],
        name="store",
    )(*[pltpu.with_memory_space_constraint(v, pltpu.VMEM) for v in results])


def solution(mesh):
    in_specs = (
        P("ev", None, "ch"),
        P("ev", "ch"),
        P("ev", None),
        P(None, "ch"),
        P(None, "ev"),
        P(None, "ch"),
        P(),
    )
    out_specs = (P("ev", None), P(None, "ch"))
    return jax.shard_map(
        on_device, mesh=mesh, in_specs=in_specs, out_specs=out_specs, check_vma=False
    )
```
